128 devices in a mesh: seq: 16 (over y, x), tensor: 8 (over z, core).
Axes of the slice: x: 4, y: 4, z: 4, core: 2. Of those that a mesh axis runs over, the one named last changes fastest.
Arguments:
- tokens: bfloat16 [2048, 4096], P('seq'), may hold values from -8 to 8
- segment_ids: int32 [2048], replicated, may hold values from -1 to 14, as said below
- routes: int32 [2048, 2], P('seq'), may hold values from 0 to 7, all different within a row; in each aligned block of 128 rows (0 to 127, 128 to 255, ...) at most 64 rows name the same one
- owners: int32 [15], replicated, may hold values from 0 to 15
- gain_attn: float32 [4096], replicated, may hold values from 0.5 to 1.5
- w_query: bfloat16 [4096, 4096], P(None, 'tensor'), may hold values from -1 to 1
- w_kv: bfloat16 [4096, 2048], P(None, 'tensor'), may hold values from -1 to 1
- w_out: bfloat16 [4096, 4096], P('tensor'), may hold values from -0.09375 to 0.09375
- gain_moe: float32 [4096], replicated, may hold values from 0.5 to 1.5
- w_router: float32 [4096, 8], replicated, may hold values from -0.09375 to 0.09375
- w_gate: bfloat16 [4096, 65536], P(None, ('seq', 'tensor')), may hold values from -0.09375 to 0.09375
- w_up: bfloat16 [4096, 65536], P(None, ('seq', 'tensor')), may hold values from -0.09375 to 0.09375
- w_down: bfloat16 [65536, 4096], P(('seq', 'tensor')), may hold values from -0.0625 to 0.0625
Outputs:
- layer_out: bfloat16 [2048, 4096], P('seq', 'tensor')
- kv_cache: bfloat16 [32768, 2048], P('seq', 'tensor')
The draws below stay inside these ranges and needn't reach their ends.
Inputs may be any that keep to these rules, and one draw needn't show every extreme that they name: `segment_ids`: tokens 0 to 1599 form segment 0; segments 1 to 14 follow in order, each of 8 to 31 tokens; all later tokens are -1. `routes`: in each aligned block of 128 rows no expert is named by more than 64 rows; the two experts of a row differ.
All inputs are finite; a program needn't handle non-finite values.
Results may differ from the reference program's by a relative error of at most 0.014.
Values may be sent and summed in bfloat16 or wider, within the bound.
No kernel may reach another device: no remote copies, remote signals or barrier semaphores. Data moves between devices by JAX's collectives and lax.ppermute only.
A program may use at most 128 MiB of HBM per device.

```python
import math
import jax
import jax.numpy as jnp
import numpy as np
from jax import lax

D = 4096
HEADS = 32
KV_HEADS = 8
HEAD_DIM = 128
EXPERTS = 8
TOPK = 2
FF = 8192
NSHORT = 14
TOK_DEV = 128
TOKENS = 2048
LONG = 1600
MOST = 64
N_SEQ = 16
N_TENSOR = 8


def draw_segment_ids(key, part):
    lengths = jax.random.randint(key, (NSHORT,), 8, 32, dtype=jnp.int32)
    ends = LONG + jnp.cumsum(lengths)
    index = jnp.arange(TOKENS, dtype=jnp.int32)
    later = 1 + jnp.sum((index[:, None] >= ends[None, :]).astype(jnp.int32), axis=1)
    labels = jnp.where(index < LONG, 0, later)
    return jnp.where(labels > NSHORT, -1, labels).astype(jnp.int32)


def draw_tokens(key, part):
    noise = jnp.clip(jax.random.normal(jax.random.fold_in(key, 10), (TOKENS, D), jnp.float32), -6.0, 6.0)
    return noise.astype(jnp.bfloat16)


def draw_w_query(key, part):
    columns = HEADS * HEAD_DIM
    bound = 6.0 / math.sqrt(D)
    base = jax.random.normal(jax.random.fold_in(key, 21), (D, columns), jnp.float32) / math.sqrt(D)
    return jnp.clip(base, -bound, bound).astype(jnp.bfloat16)


def draw_w_kv(key, part):
    columns = 2 * KV_HEADS * HEAD_DIM
    bound = 6.0 / math.sqrt(D)
    base = jax.random.normal(jax.random.fold_in(key, 22), (D, columns), jnp.float32) / math.sqrt(D)
    return jnp.clip(base, -bound, bound).astype(jnp.bfloat16)


def plant(values, rng, least, top_value):
    dims = values.shape
    place = [jax.random.randint(jax.random.fold_in(rng, axis), (), 0, dims[axis]) for axis in range(len(dims))]
    values = values.at[tuple(place)].set(least)
    longest = dims.index(max(dims))
    place[longest] = (place[longest] + 1) % dims[longest]
    return values.at[tuple(place)].set(top_value)


def steps_of(rng, dims, split, low, high):
    loudness = 1.0
    for dim, blocks in split:
        draws = jax.random.uniform(jax.random.fold_in(jax.random.fold_in(rng, 6), dim), (blocks,), jnp.float32, low / len(split), high / len(split))
        loudness = loudness * jnp.repeat(jnp.exp(draws), dims[dim] // blocks).reshape((-1,) + (1,) * (len(dims) - 1 - dim))
    return loudness


def shared_out(key, own, number, rows, count, top, limit, lean):
    order = jax.random.permutation(key, count)
    crowded, common = load_shares(count, rows * top, limit, lean, True), load_shares(count, rows * top, limit, lean, False)
    places = jnp.arange(count)

    def named(tallies, offset_by):
        used = int((tallies > 0).sum())
        fixed = max(1, used // 4)
        moved = fixed + (places - fixed + offset_by * (used - fixed)) % max(1, count - fixed)
        return jnp.zeros((count,), jnp.int32).at[order[jnp.where(places < fixed, places, moved)]].set(jnp.asarray(tallies, jnp.int32))

    tallies = jnp.where(number % 4 == 0, named(crowded, number // 4), named(common, number - number // 4 - 1))
    mixed = jax.random.permutation(jax.random.fold_in(own, 3), count)
    source_of, receiver = mixed[0:count // 2 * 2:2], mixed[1:count // 2 * 2:2]
    margin = jnp.minimum(tallies[source_of] - 1, limit - tallies[receiver]) // 2
    margin = jnp.where((source_of == order[0]) | (receiver == order[0]) | (tallies[receiver] == 0), 0, jnp.maximum(margin, 0))
    moved = jax.random.randint(jax.random.fold_in(own, 4), (count // 2,), 0, 1 << 20) % (margin + 1)
    tallies = tallies.at[source_of].add(-moved).at[receiver].add(moved)
    items = jnp.searchsorted(jnp.cumsum(tallies), jnp.arange(rows * top), side="right").astype(jnp.int32)
    grid = items.reshape(top, rows).T
    grid = grid[jax.random.permutation(jax.random.fold_in(own, 1), rows)]
    offset_by = jax.random.randint(jax.random.fold_in(own, 2), (rows, 1), 0, top)
    return jnp.take_along_axis(grid, (jnp.arange(top)[None, :] + offset_by) % top, axis=1)


def load_shares(count, total, most, lean, full):
    portions = [(1 << 20) // math.isqrt(standing ** lean) + 1 for standing in range(1, count + 1)]
    largest = most if full else min(most, max(-(-total // count), total * portions[0] // sum(portions)))
    least = 1 if total - largest >= count - 1 else 0
    given, rest = [largest] + [least] * (count - 1), total - largest - least * (count - 1)
    while rest > 0:
        movable = [i for i in range(1, count) if given[i] < largest] or [i for i in range(1, count) if given[i] < most]
        mass, budget = sum([portions[i] for i in movable]), rest
        for i in movable:
            more = min(most - given[i], max(1, budget * portions[i] // mass), rest)
            given[i] = given[i] + more
            rest = rest - more
    return np.array(given)


def centred(own_key, extent, deviation, most, cuts=(), kind=jnp.bfloat16):
    values = jax.random.normal(own_key, extent, jnp.float32) * deviation
    if len(cuts) > 0:
        values = steps_of(own_key, extent, cuts, -0.22, 0.18) * values
    return jnp.clip(values, min=-most, max=most).astype(kind)


def setup_inputs(seed: int = 0) -> dict:
    splits = jax.random.split(jax.random.key(seed), 14)
    tokens = draw_tokens(jax.random.fold_in(splits[13], 71), 0)
    segment_ids = draw_segment_ids(jax.random.fold_in(splits[13], 71), 0)
    routes_keys = jax.random.split(jax.random.fold_in(splits[2], 1), TOKENS // TOK_DEV)
    routes_turns = jax.random.permutation(jax.random.fold_in(splits[2], 3), TOKENS // TOK_DEV)
    routes = jax.vmap(lambda own, number: shared_out(jax.random.fold_in(splits[2], 2), own, number, TOK_DEV, EXPERTS, TOPK, MOST, 2))(routes_keys, routes_turns).reshape((TOKENS, TOPK))
    owners = plant(jax.random.randint(splits[3], (NSHORT + 1,), 0, N_SEQ), jax.random.fold_in(splits[3], 1), 0, N_SEQ - 1).astype(jnp.int32)
    gain_attn = jnp.clip(1.0 + 0.1 * jax.random.normal(splits[4], (D,), jnp.float32), 0.5, 1.5)
    w_query = draw_w_query(jax.random.fold_in(splits[13], 71), 0)
    w_kv = draw_w_kv(jax.random.fold_in(splits[13], 71), 0)
    w_out = centred(splits[7], (HEADS * HEAD_DIM, D), (HEADS * HEAD_DIM) ** -0.5, 0.09375, ((0, 8),))
    gain_moe = jnp.clip(1.0 + 0.1 * jax.random.normal(splits[8], (D,), jnp.float32), 0.5, 1.5)
    w_router = centred(splits[9], (D, EXPERTS), D ** -0.5, 0.09375, (), jnp.float32)
    w_gate = centred(splits[10], (D, EXPERTS * FF), D ** -0.5, 0.09375, ((1, 128),))
    w_up = centred(splits[11], (D, EXPERTS * FF), D ** -0.5, 0.09375, ((1, 128),))
    w_down = centred(splits[12], (EXPERTS * FF, D), FF ** -0.5, 0.0625, ((0, 128),))
    return {"tokens": tokens, "segment_ids": segment_ids, "routes": routes, "owners": owners, "gain_attn": gain_attn, "w_query": w_query, "w_kv": w_kv, "w_out": w_out, "gain_moe": gain_moe, "w_router": w_router, "w_gate": w_gate, "w_up": w_up, "w_down": w_down}


EPS = 1e-05
THETA = 1000000.0
FLOOR = -1e+30

def settle(value):
    return lax.optimization_barrier(value.astype(jnp.bfloat16)).astype(jnp.float32)

def rms_norm(rows, gain):
    values = rows.astype(jnp.float32)
    scale = lax.rsqrt(lax.optimization_barrier(jnp.mean(values * values, axis=-1, keepdims=True)) + EPS)
    return (values * scale * gain).astype(jnp.bfloat16)

def rotate(values, position):
    half = values.shape[-1] // 2
    freqs = THETA ** (-(jnp.arange(half, dtype=jnp.float32) * 2.0) / values.shape[-1])
    angles = position.astype(jnp.float32)[:, None] * freqs[None, :]
    cosine = jnp.cos(angles)[:, None, :]
    sine = jnp.sin(angles)[:, None, :]
    first = values[..., :half]
    second = values[..., half:]
    return jnp.concatenate([first * cosine - second * sine, second * cosine + first * sine], axis=-1)

def segment_layout(segment_ids, owners):
    short_count = owners.shape[0] - 1
    labels = jnp.where(segment_ids < 0, short_count + 1, segment_ids).astype(jnp.int32)
    onehot = labels[:, None] == jnp.arange(short_count + 2, dtype=jnp.int32)[None, :]
    counts = lax.optimization_barrier(jnp.sum(onehot.astype(jnp.int32), axis=0)).astype(jnp.int32)
    starts = (jnp.cumsum(counts) - counts).astype(jnp.int32)
    seg_start = lax.optimization_barrier(jnp.sum(jnp.where(onehot, starts[None, :], 0), axis=1)).astype(jnp.int32)
    owner_ext = jnp.concatenate([owners.astype(jnp.int32), jnp.full((1,), -1, jnp.int32)])
    owner_tok = lax.optimization_barrier(jnp.sum(jnp.where(onehot, owner_ext[None, :], 0), axis=1)).astype(jnp.int32)
    return (seg_start, owner_tok)

def owner_slots(owner_tok, owner_count):
    hits = (owner_tok[:, None] == jnp.arange(owner_count, dtype=jnp.int32)[None, :]).astype(jnp.int32)
    before = jnp.cumsum(hits, axis=0) - hits
    return lax.optimization_barrier(jnp.sum(before * hits, axis=1)).astype(jnp.int32)

def reference(tokens, segment_ids, routes, owners, gain_attn, w_query, w_kv, w_out, gain_moe, w_router, w_gate, w_up, w_down):
    seg_start, owner_tok = segment_layout(segment_ids, owners)
    index = jnp.arange(TOKENS, dtype=jnp.int32)
    position = index - seg_start
    normed = rms_norm(tokens, gain_attn)
    queries = jnp.dot(normed, w_query, preferred_element_type=jnp.float32).reshape(TOKENS, HEADS, HEAD_DIM)
    queries = rotate(queries, position).astype(jnp.bfloat16)
    pairs = jnp.dot(normed, w_kv, preferred_element_type=jnp.float32).reshape(TOKENS, KV_HEADS, 2, HEAD_DIM)
    keys = rotate(pairs[:, :, 0], position).astype(jnp.bfloat16)
    values = pairs[:, :, 1].astype(jnp.bfloat16)
    group = HEADS // KV_HEADS
    grouped = queries.reshape(TOKENS, KV_HEADS, group, HEAD_DIM)
    allowed = (index[None, :] <= index[:, None]) & (index[None, :] >= seg_start[:, None])
    scale = HEAD_DIM ** (-0.5)

    def one_head(operands):
        query_head, key_head, value_head = operands
        scores = jnp.einsum('qgd,nd->gqn', query_head.astype(jnp.float32), key_head.astype(jnp.float32)) * scale
        scores = jnp.where(allowed[None], scores, FLOOR)
        top = lax.optimization_barrier(jnp.max(scores, axis=-1, keepdims=True))
        weights = jnp.where(allowed[None], jnp.exp(scores - top), 0.0)
        total = lax.optimization_barrier(jnp.sum(weights, axis=-1))
        mixed = jnp.einsum('gqn,nd->gqd', settle(weights), value_head.astype(jnp.float32))
        return mixed / total[..., None]
    heads_out = lax.map(one_head, (grouped.transpose(1, 0, 2, 3), keys.transpose(1, 0, 2), values.transpose(1, 0, 2)))
    attended = heads_out.transpose(2, 0, 1, 3).reshape(TOKENS, HEADS * HEAD_DIM).astype(jnp.bfloat16)
    attn_out = jnp.dot(attended, w_out, preferred_element_type=jnp.float32)
    residual = (tokens.astype(jnp.float32) + attn_out).astype(jnp.bfloat16)
    moe_in = rms_norm(residual, gain_moe)
    logits = jnp.dot(moe_in.astype(jnp.float32), w_router, preferred_element_type=jnp.float32)
    expert_ids = jnp.arange(EXPERTS, dtype=jnp.int32)
    picked = routes[:, :, None] == expert_ids[None, None, :]
    chosen = lax.optimization_barrier(jnp.sum(jnp.where(picked, logits[:, None, :], 0.0), axis=2))
    gates = jax.nn.softmax(chosen, axis=1)
    holders = N_SEQ // EXPERTS
    block = FF // (holders * N_TENSOR)
    bound = N_SEQ * MOST
    padded = jnp.concatenate([moe_in, jnp.zeros((1, D), jnp.bfloat16)], axis=0)

    def add_expert(expert, mixture):
        wg = lax.dynamic_slice_in_dim(w_gate, expert * FF, FF, 1)
        wu = lax.dynamic_slice_in_dim(w_up, expert * FF, FF, 1)
        wd = lax.dynamic_slice_in_dim(w_down, expert * FF, FF, 0)
        hit = jnp.any(routes == expert, axis=1)
        chosen_rows = jnp.nonzero(hit, size=bound, fill_value=TOKENS)[0].astype(jnp.int32)
        rows_in = padded[chosen_rows]
        active = (jax.nn.silu(jnp.dot(rows_in, wg, preferred_element_type=jnp.float32)) * jnp.dot(rows_in, wu, preferred_element_type=jnp.float32)).astype(jnp.bfloat16)
        result = jnp.zeros((bound, D), jnp.float32)
        for holder in range(holders):
            group_sum = jnp.zeros((bound, D), jnp.float32)
            for member in range(N_TENSOR):
                low = (holder * N_TENSOR + member) * block
                group_sum = group_sum + settle(jnp.dot(active[:, low:low + block], wd[low:low + block], preferred_element_type=jnp.float32))
            result = result + settle(group_sum)
        weight = lax.optimization_barrier(jnp.sum(jnp.where(routes == expert, gates, 0.0), axis=1))
        spread = jnp.zeros((TOKENS + 1, D), jnp.float32).at[chosen_rows].set(result)[:TOKENS]
        return mixture + weight[:, None] * spread
    mixture = lax.fori_loop(0, EXPERTS, add_expert, jnp.zeros((TOKENS, D), jnp.float32))
    layer_out = (residual.astype(jnp.float32) + mixture).astype(jnp.bfloat16)
    kv_rows = jnp.stack([keys, values], axis=2).reshape(TOKENS, 2 * KV_HEADS * HEAD_DIM)
    slots = owner_slots(owner_tok, N_SEQ)
    target = jnp.where(owner_tok >= 0, owner_tok * TOKENS + slots, N_SEQ * TOKENS).astype(jnp.int32)
    kv_cache = jnp.zeros((N_SEQ * TOKENS + 1, 2 * KV_HEADS * HEAD_DIM), jnp.bfloat16).at[target].set(kv_rows)[:N_SEQ * TOKENS]
    return (layer_out, kv_cache)
```

```python
import jax
import jax.numpy as jnp
from jax import lax
from jax.experimental import pallas as pl
from jax.experimental.pallas import tpu as pltpu
from jax.sharding import PartitionSpec as P

HEADS = 32
KV_HEADS = 8
HEAD_DIM = 128
EXPERTS = 8
EPS = 1e-05
THETA = 1000000.0
FLOOR = -1e30
NY = 4
NX = 4
NZ = 4
F32 = jnp.float32
BF16 = jnp.bfloat16


VMEM_SPEC = pl.BlockSpec(memory_space=pltpu.VMEM)
SMEM_SPEC = pl.BlockSpec(memory_space=pltpu.SMEM)


def z_perm(step):
    return [(2 * z + c, 2 * ((z + step) % NZ) + c) for z in range(NZ) for c in range(2)]


def core_perm():
    return [(t, t ^ 1) for t in range(2 * NZ)]


def x_perm(step):
    return [(NX * y + x, NX * y + (x + step) % NX) for y in range(NY) for x in range(NX)]


def y_perm(step):
    return [(NX * y + x, NX * ((y + step) % NY) + x) for y in range(NY) for x in range(NX)]


def send_z(value, step):
    return lax.ppermute(value, "tensor", z_perm(step))


def send_core(value):
    return lax.ppermute(value, "tensor", core_perm())


def rotate(values, cosine, sine):
    half = values.shape[-1] // 2
    first = values[..., :half]
    second = values[..., half:]
    return jnp.concatenate(
        [first * cosine - second * sine, second * cosine + first * sine], axis=-1
    )


def join_kernel(*refs):
    out = refs[-1]
    rows = refs[0].shape[0]
    for i, ref in enumerate(refs[:-1]):
        out[i * rows : (i + 1) * rows, :] = ref[...]


def join(parts):
    rows, cols = parts[0].shape
    return pl.pallas_call(
        join_kernel,
        out_shape=jax.ShapeDtypeStruct((rows * len(parts), cols), parts[0].dtype),
        in_specs=[VMEM_SPEC] * len(parts),
        out_specs=VMEM_SPEC,
    )(*parts)


def attention_kernel(place, q_ref, start_ref, *refs):
    out_ref = refs[-1]
    pieces = refs[:-1]
    rows, dim = start_ref.shape[0], HEAD_DIM
    group = q_ref.shape[0] // rows
    y = place[0]
    x = place[1]
    first = (y * NX + x) * rows
    count = pieces[0].shape[0]
    query = first + lax.broadcasted_iota(jnp.int32, (rows, count), 0)
    column = lax.broadcasted_iota(jnp.int32, (rows, count), 1)
    block = column // rows
    inner = column - block * rows
    block_x = lax.rem(x - block + NX, NX)
    start = start_ref[...]
    scale = HEAD_DIM ** (-0.5)
    masks = []
    for dy in range(NY):
        block_y = lax.rem(y - dy + NY, NY)
        key = (block_y * NX + block_x) * rows + inner
        masks.append((key <= query) & (key >= start))
    for g in range(group):
        q = q_ref[g * rows : (g + 1) * rows, :]
        scores = []
        top = jnp.full((rows, 1), FLOOR, F32)
        for dy in range(NY):
            s = lax.dot_general(
                q, pieces[dy][:, :dim], (((1,), (1,)), ((), ())), preferred_element_type=F32
            )
            s = jnp.where(masks[dy], s * scale, FLOOR)
            top = jnp.maximum(top, jnp.max(s, axis=1, keepdims=True))
            scores.append(s)
        mass = jnp.zeros((rows, 1), F32)
        acc = jnp.zeros((rows, dim), F32)
        for dy in range(NY):
            w = jnp.where(masks[dy], jnp.exp(scores[dy] - top), 0.0)
            mass = mass + jnp.sum(w, axis=1, keepdims=True)
            acc = acc + jnp.dot(
                w.astype(BF16), pieces[dy][:, dim:], preferred_element_type=F32
            )
        out_ref[:, g * dim : (g + 1) * dim] = (acc / mass).astype(BF16)


def attend(place, q, start, pieces):
    rows = start.shape[0]
    width = q.shape[0] // rows * HEAD_DIM
    return pl.pallas_call(
        attention_kernel,
        out_shape=jax.ShapeDtypeStruct((rows, width), BF16),
        in_specs=[SMEM_SPEC] + [VMEM_SPEC] * (2 + len(pieces)),
        out_specs=VMEM_SPEC,
    )(place, q, start, *pieces)


def out_kernel(ids, a_ref, w_ref, o_ref):
    o_ref[0] = jnp.dot(a_ref[...], w_ref[...], preferred_element_type=F32).astype(BF16)


def project_out(ids, attended, w_out, share):
    rows, depth = attended.shape
    count = ids.shape[0]
    return pl.pallas_call(
        out_kernel,
        out_shape=jax.ShapeDtypeStruct((count, rows, share), BF16),
        grid_spec=pltpu.PrefetchScalarGridSpec(
            num_scalar_prefetch=1,
            grid=(count,),
            in_specs=[
                pl.BlockSpec((rows, depth), lambda i, ids: (0, 0)),
                pl.BlockSpec((depth, share), lambda i, ids: (0, ids[i])),
            ],
            out_specs=pl.BlockSpec((1, rows, share), lambda i, ids: (i, 0, 0)),
        ),
    )(ids, attended, w_out)


def ffn_kernel(ids, gain_ref, wg_ref, wu_ref, wd_ref, *refs):
    pieces = refs[:10]
    mine_ref, far_ref, other_ref = refs[10:13]
    xs_ref = refs[13]
    rows, share = pieces[0].shape
    half = rows // 2
    width = wg_ref.shape[0]
    placed = [(pieces[k], 0, ids[k]) for k in range(6)]
    placed += [(pieces[6], 0, ids[6]), (pieces[7], half, ids[6])]
    placed += [(pieces[8], 0, ids[7]), (pieces[9], half, ids[7])]
    tile = 64
    for r in range(0, rows, tile):
        total = jnp.zeros((tile, share), F32)
        for ref, low, _ in placed:
            if low <= r < low + ref.shape[0]:
                v = ref[r - low : r - low + tile, :].astype(F32)
                total = total + v * v
        mean = jnp.sum(total, axis=1, keepdims=True) * (1.0 / width)
        scale = lax.rsqrt(mean + EPS)
        for ref, low, at in placed:
            if low <= r < low + ref.shape[0]:
                v = ref[r - low : r - low + tile, :].astype(F32)
                v = (v * scale * gain_ref[pl.ds(at, 1), :]).astype(BF16)
                xs_ref[r : r + tile, pl.ds(pl.multiple_of(at * share, share), share)] = v
    gate = jnp.dot(xs_ref[...], wg_ref[...], preferred_element_type=F32)
    up = jnp.dot(xs_ref[...], wu_ref[...], preferred_element_type=F32)
    active = (gate / (1.0 + jnp.exp(-gate)) * up).astype(BF16)

    def down(at):
        w = wd_ref[:, pl.ds(pl.multiple_of(at * share, share), share)]
        return jnp.dot(active, w, preferred_element_type=F32).astype(BF16)

    far_ref[...] = down(ids[14])
    for i, d in enumerate((1, 3, 0)):
        other_ref[i] = down(ids[12 + d])
    for d in range(4):
        mine_ref[d] = down(ids[8 + d])


def ffn(ids, gain, w_gate, w_up, w_down, pieces):
    rows, share = pieces[0].shape
    return pl.pallas_call(
        ffn_kernel,
        out_shape=(
            jax.ShapeDtypeStruct((4, rows, share), BF16),
            jax.ShapeDtypeStruct((rows, share), BF16),
            jax.ShapeDtypeStruct((3, rows, share), BF16),
        ),
        in_specs=[SMEM_SPEC] + [VMEM_SPEC] * (4 + len(pieces)),
        out_specs=(VMEM_SPEC,) * 3,
        scratch_shapes=[pltpu.VMEM((rows, w_gate.shape[0]), BF16)],
        compiler_params=pltpu.CompilerParams(vmem_limit_bytes=56 * 1024 * 1024),
    )(ids, gain, w_gate, w_up, w_down, *pieces)


def gather_ring(own):
    half = own.shape[0] // 2
    below = send_z(own, 1)
    above = send_z(own, -1)
    far_a = send_z(below[:half], 1)
    far_b = send_z(above[half:], -1)
    own_s = send_core(own)
    below_s = send_core(below)
    above_s = send_core(above)
    far_as = send_core(far_a)
    far_bs = send_core(far_b)
    return [own, own_s, below, below_s, above, above_s, far_a, far_b, far_as, far_bs]


def add(*parts):
    total = parts[0].astype(F32)
    for part in parts[1:]:
        total = total + part.astype(F32)
    return total.astype(BF16)


def scatter_ring(mine, far, other):
    half = far.shape[0] // 2
    far_r = send_core(far)
    other_r = send_core(other)
    far_sum = add(mine[2], far_r)
    in_a = send_z(far_sum[:half], 1)
    in_b = send_z(far_sum[half:], -1)
    next_b = add(mine[1][half:], other_r[0][half:])
    prev_a = add(mine[3][:half], other_r[1][:half])
    from_below_b = send_z(next_b, 1)
    from_above_a = send_z(prev_a, -1)
    next_a = add(mine[1][:half], other_r[0][:half], in_a)
    prev_b = add(mine[3][half:], other_r[1][half:], in_b)
    from_below_a = send_z(next_a, 1)
    from_above_b = send_z(prev_b, -1)
    top = add(mine[0][:half], other_r[2][:half], from_below_a, from_above_a)
    low = add(mine[0][half:], other_r[2][half:], from_below_b, from_above_b)
    return top, low


def local(
    tokens,
    segment_ids,
    routes,
    owners,
    gain_attn,
    w_query,
    w_kv,
    w_out,
    gain_moe,
    w_router,
    w_gate,
    w_up,
    w_down,
):
    seq_count = lax.axis_size("seq")
    ten_count = lax.axis_size("tensor")
    seq_rank = lax.axis_index("seq").astype(jnp.int32)
    ten_rank = lax.axis_index("tensor").astype(jnp.int32)
    rows, width = tokens.shape
    total = segment_ids.shape[0]
    share = width // ten_count
    group = HEADS // KV_HEADS
    y = seq_rank // NX
    x = seq_rank - y * NX
    z = ten_rank // 2
    c = ten_rank - z * 2
    first = seq_rank * rows

    short_count = owners.shape[0] - 1
    labels = jnp.where(segment_ids < 0, short_count + 1, segment_ids)
    my_labels = lax.dynamic_slice_in_dim(labels, first, rows)
    seg_start = jnp.sum((labels[None, :] < my_labels[:, None]).astype(jnp.int32), axis=1)
    position = first + jnp.arange(rows, dtype=jnp.int32) - seg_start

    values = tokens.astype(F32)
    scale = lax.rsqrt(jnp.mean(values * values, axis=-1, keepdims=True) + EPS)
    normed = (values * scale * gain_attn).astype(BF16)
    half_dim = HEAD_DIM // 2
    freqs = THETA ** (-(jnp.arange(half_dim, dtype=F32) * 2.0) / HEAD_DIM)
    angles = position.astype(F32)[:, None] * freqs[None, :]
    cosine = jnp.cos(angles)
    sine = jnp.sin(angles)
    pairs = jnp.dot(normed, w_kv, preferred_element_type=F32)
    keys = rotate(pairs[:, :HEAD_DIM], cosine, sine).astype(BF16)
    kv_own = jnp.concatenate([keys, pairs[:, HEAD_DIM:].astype(BF16)], axis=1)
    queries = jnp.dot(normed, w_query, preferred_element_type=F32)
    q = jnp.concatenate(
        [
            rotate(queries[:, g * HEAD_DIM : (g + 1) * HEAD_DIM], cosine, sine).astype(BF16)
            for g in range(group)
        ],
        axis=0,
    )

    row_parts = [kv_own] + [lax.ppermute(kv_own, "seq", x_perm(d)) for d in range(1, NX)]
    kv_row = join(row_parts)
    kv_pieces = [kv_row] + [lax.ppermute(kv_row, "seq", y_perm(d)) for d in range(1, NY)]
    place = jnp.stack([y, x])
    attended = attend(place, q, seg_start[:, None], kv_pieces)

    turn = jnp.arange(NZ, dtype=jnp.int32)
    ring = lax.rem(z + turn, NZ) * 2
    other_c = 1 - c
    out_sib = project_out(ring + other_c, attended, w_out, share)
    out_sib_r = send_core(out_sib)
    out_mine = project_out(ring + c, attended, w_out, share)
    sums = [out_mine[d].astype(F32) + out_sib_r[d].astype(F32) for d in range(NZ)]
    attn_sum = sums[0]
    for d in range(1, NZ):
        attn_sum = attn_sum + send_z(sums[d].astype(BF16), d).astype(F32)
    own_tokens = lax.dynamic_slice_in_dim(tokens, ten_rank * share, share, 1)
    residual = (own_tokens.astype(F32) + attn_sum).astype(BF16)

    capacity = rows // 2
    slots = capacity // 2
    holders = seq_count // EXPERTS
    expert_ids = jnp.arange(EXPERTS, dtype=jnp.int32)
    hit = (routes[:, 0:1] == expert_ids[None, :]) | (routes[:, 1:2] == expert_ids[None, :])
    index = jnp.arange(rows, dtype=jnp.int32)
    before = (index[:, None] > index[None, :]).astype(BF16)
    rank = jnp.dot(before, hit.astype(BF16), preferred_element_type=F32).astype(jnp.int32)
    slot_of = jnp.where(hit, rank, -1)
    slot_dup = jnp.repeat(slot_of.T, holders, axis=0)

    def pack(low):
        want = low + jnp.arange(slots, dtype=jnp.int32)
        return slot_dup[:, None, :] == want[None, :, None]

    picks = [pack(0), pack(slots)]

    def dispatch(pick):
        flat = pick.reshape(seq_count * slots, rows).astype(BF16)
        out = jnp.dot(flat, residual, preferred_element_type=F32).astype(BF16)
        got = lax.all_to_all(out.reshape(seq_count, slots, share), "seq", 0, 0, tiled=True)
        return got.reshape(seq_count * slots, share)

    gain_share = lax.dynamic_slice_in_dim(gain_moe, ten_rank * share, share)
    router = lax.dynamic_slice_in_dim(w_router, ten_rank * share, share)
    res32 = residual.astype(F32)
    part = jnp.dot(
        res32 * gain_share, router, preferred_element_type=F32, precision=lax.Precision.HIGHEST
    )
    square = jnp.sum(res32 * res32, axis=1, keepdims=True)
    stats = jnp.concatenate([part, square, jnp.zeros((rows, 7), F32)], axis=1)
    stats = stats + send_core(stats)
    stats = stats + lax.ppermute(stats, "tensor", [(t, t ^ 2) for t in range(ten_count)])
    stats = stats + lax.ppermute(stats, "tensor", [(t, t ^ 4) for t in range(ten_count)])
    logits = stats[:, :EXPERTS] * lax.rsqrt(stats[:, EXPERTS : EXPERTS + 1] / width + EPS)
    picked = routes[:, :, None] == expert_ids[None, None, :]
    chosen = jnp.sum(jnp.where(picked, logits[:, None, :], 0.0), axis=2)
    gates = jax.nn.softmax(chosen, axis=1)
    gate_of = jnp.sum(jnp.where(picked, gates[:, :, None], 0.0), axis=1)
    gate_dup = jnp.repeat(gate_of, holders, axis=1)

    gain_rows = gain_moe.reshape(ten_count, share)
    prev_z = lax.rem(z + NZ - 1, NZ) * 2
    next_z = lax.rem(z + 1, NZ) * 2
    far_z = lax.rem(z + 2, NZ) * 2
    base = z * 2
    ids = jnp.concatenate(
        [
            jnp.stack([v + k for v in (base, prev_z, next_z, far_z) for k in (c, other_c)]),
            ring + c,
            ring + other_c,
        ]
    )
    a_own = dispatch(picks[0])
    b_own = dispatch(picks[1])
    a_pieces = gather_ring(a_own)
    b_pieces = gather_ring(b_own)
    a_out = ffn(ids, gain_rows, w_gate, w_up, w_down, a_pieces)
    b_out = ffn(ids, gain_rows, w_gate, w_up, w_down, b_pieces)

    def give_back(parts):
        flat = jnp.concatenate(parts, axis=0)
        got = lax.all_to_all(flat.reshape(seq_count, slots, share), "seq", 0, 0, tiled=True)
        return got.reshape(seq_count * slots, share)

    a_back = give_back(scatter_ring(*a_out))
    b_back = give_back(scatter_ring(*b_out))

    def combine(pick, back):
        weight = jnp.where(pick.transpose(2, 0, 1), gate_dup[:, :, None], 0.0)
        weight = weight.reshape(rows, seq_count * slots)
        high = weight.astype(BF16)
        low = (weight - high.astype(F32)).astype(BF16)
        return jnp.dot(high, back, preferred_element_type=F32) + jnp.dot(
            low, back, preferred_element_type=F32
        )

    mixture = combine(picks[0], a_back) + combine(picks[1], b_back)
    layer_out = (res32 + mixture).astype(BF16)

    owner_ext = jnp.concatenate([owners, jnp.full((1,), -1, jnp.int32)])
    label_ids = jnp.arange(short_count + 2, dtype=jnp.int32)
    owner_tok = jnp.sum(
        jnp.where(labels[:, None] == label_ids[None, :], owner_ext[None, :], 0), axis=1
    )
    held = (owner_tok == seq_rank).reshape(seq_count, rows)
    held_b = held.astype(BF16)
    inside = jnp.dot(held_b, before.T, preferred_element_type=F32)
    seq_index = jnp.arange(seq_count, dtype=jnp.int32)
    earlier = (seq_index[:, None] > seq_index[None, :]).astype(BF16)
    sizes = jnp.sum(held.astype(F32), axis=1).astype(BF16)
    ahead = jnp.dot(earlier, sizes[:, None], preferred_element_type=F32)
    slot = jnp.where(held, (inside + ahead).astype(jnp.int32), -1).reshape(NY, NX, rows)
    turned = slot[:, ::-1][::-1]
    turned = jnp.concatenate([turned, turned], axis=0)
    turned = lax.dynamic_slice_in_dim(turned, NY - 1 - y, NY, 0)
    turned = jnp.concatenate([turned, turned], axis=1)
    turned = lax.dynamic_slice_in_dim(turned, NX - 1 - x, NX, 1)
    places = jnp.arange(total, dtype=jnp.int32)
    cache = jnp.zeros((total, kv_own.shape[1]), F32)
    for dy in range(NY):
        take = (places[:, None] == turned[dy].reshape(1, NX * rows)).astype(BF16)
        cache = cache + jnp.dot(take, kv_pieces[dy], preferred_element_type=F32)
    return layer_out, cache.astype(BF16)


def solution(mesh):
    return jax.shard_map(
        local,
        mesh=mesh,
        in_specs=(
            P("seq", None),
            P(),
            P("seq", None),
            P(),
            P(),
            P(None, "tensor"),
            P(None, "tensor"),
            P("tensor", None),
            P(),
            P(),
            P(None, ("seq", "tensor")),
            P(None, ("seq", "tensor")),
            P(("seq", "tensor"), None),
        ),
        out_specs=(P("seq", "tensor"), P("seq", "tensor")),
        check_vma=False,
    )
```

```python
import jax
import jax.numpy as jnp
from jax import lax
from jax.experimental import pallas as pl
from jax.experimental.pallas import tpu as pltpu
from jax.sharding import PartitionSpec as P


HEADS = 32
KV_HEADS = 8
HEAD_DIM = 128
EXPERTS = 8
EPS = 1e-05
THETA = 1000000.0
FLOOR = -1e30
NZ = 4
MIB = 1024 * 1024
F32 = jnp.float32
BF16 = jnp.bfloat16


VMEM_SPEC = pl.BlockSpec(memory_space=pltpu.VMEM)
ANY_SPEC = pl.BlockSpec(memory_space=pl.ANY)
SMEM_SPEC = pl.BlockSpec(memory_space=pltpu.SMEM)


def z_perm(step):
    return [(2 * z + c, 2 * ((z + step) % NZ) + c) for z in range(NZ) for c in range(2)]


def core_perm():
    return [(t, t ^ 1) for t in range(2 * NZ)]


def send_z(value, step):
    return lax.ppermute(value, "tensor", z_perm(step))


def send_core(value):
    return lax.ppermute(value, "tensor", core_perm())


def rotate(values, cosine, sine):
    half = values.shape[-1] // 2
    first = values[..., :half]
    second = values[..., half:]
    return jnp.concatenate(
        [first * cosine - second * sine, second * cosine + first * sine], axis=-1
    )


def attention_kernel(ids, first_ref, q_ref, start_ref, kv_ref, w_hbm, mine_ref, sib_ref, w_ref, sem):
    copy = pltpu.make_async_copy(w_hbm, w_ref, sem)
    copy.start()
    rows, dim = start_ref.shape[0], HEAD_DIM
    group = q_ref.shape[0] // rows
    count = kv_ref.shape[0]
    query = first_ref[0] + lax.broadcasted_iota(jnp.int32, (rows, count), 0)
    key = lax.broadcasted_iota(jnp.int32, (rows, count), 1)
    mask = (key <= query) & (key >= start_ref[...])
    scale = HEAD_DIM ** (-0.5)
    heads = []
    for g in range(group):
        q = q_ref[g * rows : (g + 1) * rows, :]
        s = lax.dot_general(
            q, kv_ref[:, :dim], (((1,), (1,)), ((), ())), preferred_element_type=F32
        )
        s = jnp.where(mask, s * scale, FLOOR)
        w = jnp.where(mask, jnp.exp(s - jnp.max(s, axis=1, keepdims=True)), 0.0)
        mass = jnp.sum(w, axis=1, keepdims=True)
        acc = jnp.dot(w.astype(BF16), kv_ref[:, dim:], preferred_element_type=F32)
        heads.append((acc / mass).astype(BF16))
    attended = jnp.concatenate(heads, axis=1)
    copy.wait()
    share = mine_ref.shape[2]

    def project(at):
        w = w_ref[:, pl.ds(pl.multiple_of(at * share, share), share)]
        return jnp.dot(attended, w, preferred_element_type=F32)

    def body(d, carry):
        sib_ref[d] = project(ids[4 + d]).astype(BF16)
        mine_ref[d] = project(ids[d])
        return carry

    lax.fori_loop(0, NZ, body, 0)


def attend(ids, first, q, start, kv, w_out, share):
    rows = start.shape[0]
    return pl.pallas_call(
        attention_kernel,
        out_shape=(
            jax.ShapeDtypeStruct((NZ, rows, share), F32),
            jax.ShapeDtypeStruct((NZ, rows, share), BF16),
        ),
        in_specs=[SMEM_SPEC, SMEM_SPEC, VMEM_SPEC, VMEM_SPEC, VMEM_SPEC, ANY_SPEC],
        out_specs=(VMEM_SPEC, VMEM_SPEC),
        scratch_shapes=[pltpu.VMEM(w_out.shape, BF16), pltpu.SemaphoreType.DMA],
        compiler_params=pltpu.CompilerParams(vmem_limit_bytes=24 * MIB),
    )(ids, first, q, start, kv, w_out)


def ffn_kernel(ids, gain_ref, wg_hbm, wu_hbm, wd_hbm, *refs):
    pieces = refs[:8]
    mine_ref, sib_ref = refs[-9:-7]
    xs_ref, act_ref, wg_ref, wu_ref, wd_ref, sems, _ = refs[-7:]
    copies = [
        pltpu.make_async_copy(hbm, ref, sems.at[i])
        for i, (hbm, ref) in enumerate(((wg_hbm, wg_ref), (wu_hbm, wu_ref), (wd_hbm, wd_ref)))
    ]
    for copy in copies:
        copy.start()
    rows, share = pieces[0].shape
    width = wg_ref.shape[0]
    tile = 32

    def norm(i, carry):
        at_row = pl.ds(pl.multiple_of(i * tile, tile), tile)
        total = jnp.zeros((tile, share), F32)
        for ref in pieces:
            v = ref[at_row, :].astype(F32)
            total = total + v * v
        mean = jnp.sum(total, axis=1, keepdims=True) * (1.0 / width)
        scale = lax.rsqrt(mean + EPS)
        for k, ref in enumerate(pieces):
            at = ids[k]
            v = ref[at_row, :].astype(F32) * scale * gain_ref[pl.ds(at, 1), :]
            xs_ref[at_row, pl.ds(pl.multiple_of(at * share, share), share)] = v.astype(BF16)
        return carry

    lax.fori_loop(0, rows // tile, norm, 0)
    copies[0].wait()
    copies[1].wait()
    block = 256

    def hidden(i, carry):
        at_row = pl.ds(pl.multiple_of(i * block, block), block)
        v = xs_ref[at_row, :]
        gate = jnp.dot(v, wg_ref[...], preferred_element_type=F32)
        up = jnp.dot(v, wu_ref[...], preferred_element_type=F32)
        act_ref[at_row, :] = (gate / (1.0 + jnp.exp(-gate)) * up).astype(BF16)
        return carry

    lax.fori_loop(0, rows // block, hidden, 0)
    copies[2].wait()

    def down(at):
        w = wd_ref[:, pl.ds(pl.multiple_of(at * share, share), share)]
        return jnp.dot(act_ref[...], w, preferred_element_type=F32).astype(BF16)

    def body(d, carry):
        sib_ref[d] = down(ids[12 + d])
        mine_ref[d] = down(ids[8 + d])
        return carry

    lax.fori_loop(0, NZ, body, 0)


def ffn(ids, gain, w_gate, w_up, w_down, pieces, after):
    rows, share = pieces[0].shape
    return pl.pallas_call(
        ffn_kernel,
        out_shape=(
            jax.ShapeDtypeStruct((NZ, rows, share), BF16),
            jax.ShapeDtypeStruct((NZ, rows, share), BF16),
        ),
        in_specs=[SMEM_SPEC, VMEM_SPEC]
        + [ANY_SPEC] * 3
        + [VMEM_SPEC] * len(pieces)
        + [ANY_SPEC] * len(after),
        out_specs=(VMEM_SPEC,) * 2,
        scratch_shapes=[
            pltpu.VMEM((rows, w_gate.shape[0]), BF16),
            pltpu.VMEM((rows, w_gate.shape[1]), BF16),
            pltpu.VMEM(w_gate.shape, BF16),
            pltpu.VMEM(w_up.shape, BF16),
            pltpu.VMEM(w_down.shape, BF16),
            pltpu.SemaphoreType.DMA((3,)),
            pltpu.VMEM((8, 128), F32),
        ],
        compiler_params=pltpu.CompilerParams(vmem_limit_bytes=36 * MIB),
    )(ids, gain, w_gate, w_up, w_down, *pieces, *after)


def gather_ring(own):
    ring = [own] + [send_z(own, d) for d in (1, 3, 2)]
    return ring + [send_core(v) for v in ring]


def add(*parts):
    total = parts[0].astype(F32)
    for part in parts[1:]:
        total = total + part.astype(F32)
    return total.astype(BF16)


def scatter_start(mine, sib):
    got = send_core(sib)
    return [add(mine[d], got[d]) for d in range(1, NZ)], (mine[0], got[0])


def scatter_end(sums, own):
    moved = [send_z(sums[d - 1], d) for d in (1, 3, 2)]
    return add(*own, *moved)


def local(
    tokens,
    segment_ids,
    routes,
    owners,
    gain_attn,
    w_query,
    w_kv,
    w_out,
    gain_moe,
    w_router,
    w_gate,
    w_up,
    w_down,
):
    seq_count = lax.axis_size("seq")
    ten_count = lax.axis_size("tensor")
    seq_rank = lax.axis_index("seq").astype(jnp.int32)
    ten_rank = lax.axis_index("tensor").astype(jnp.int32)
    rows, width = tokens.shape
    total = segment_ids.shape[0]
    share = width // ten_count
    group = HEADS // KV_HEADS
    z = ten_rank // 2
    c = ten_rank - z * 2
    first = seq_rank * rows

    short_count = owners.shape[0] - 1
    labels = jnp.where(segment_ids < 0, short_count + 1, segment_ids)
    my_labels = lax.dynamic_slice_in_dim(labels, first, rows)
    seg_start = jnp.sum((labels[None, :] < my_labels[:, None]).astype(jnp.int32), axis=1)
    position = first + jnp.arange(rows, dtype=jnp.int32) - seg_start

    values = tokens.astype(F32)
    scale = lax.rsqrt(jnp.mean(values * values, axis=-1, keepdims=True) + EPS)
    normed = (values * scale * gain_attn).astype(BF16)
    half_dim = HEAD_DIM // 2
    freqs = THETA ** (-(jnp.arange(half_dim, dtype=F32) * 2.0) / HEAD_DIM)
    angles = position.astype(F32)[:, None] * freqs[None, :]
    cosine = jnp.cos(angles)
    sine = jnp.sin(angles)
    pairs = jnp.dot(normed, w_kv, preferred_element_type=F32)
    keys = rotate(pairs[:, :HEAD_DIM], cosine, sine).astype(BF16)
    kv_own = jnp.concatenate([keys, pairs[:, HEAD_DIM:].astype(BF16)], axis=1)
    queries = jnp.dot(normed, w_query, preferred_element_type=F32)
    q = jnp.concatenate(
        [
            rotate(queries[:, g * HEAD_DIM : (g + 1) * HEAD_DIM], cosine, sine).astype(BF16)
            for g in range(group)
        ],
        axis=0,
    )

    kv_all = lax.all_to_all(
        jnp.broadcast_to(kv_own[None], (seq_count,) + kv_own.shape), "seq", 0, 0, tiled=True
    ).reshape(total, kv_own.shape[1])

    ring = lax.rem(z + jnp.arange(NZ, dtype=jnp.int32), NZ) * 2
    other_c = 1 - c
    out_ids = jnp.concatenate([ring + c, ring + other_c])
    out_mine, out_sib = attend(
        out_ids, first.reshape(1), q, seg_start[:, None], kv_all, w_out, share
    )
    out_sib_r = send_core(out_sib)
    sums = [out_mine[d] + out_sib_r[d].astype(F32) for d in range(NZ)]
    attn_sum = sums[0]
    for d in (1, 3, 2):
        attn_sum = attn_sum + send_z(sums[d].astype(BF16), d).astype(F32)
    own_tokens = lax.dynamic_slice_in_dim(tokens, ten_rank * share, share, 1)
    residual = (own_tokens.astype(F32) + attn_sum).astype(BF16)

    capacity = rows // 2
    slots = capacity // 2
    holders = seq_count // EXPERTS
    expert_ids = jnp.arange(EXPERTS, dtype=jnp.int32)
    hit = (routes[:, 0:1] == expert_ids[None, :]) | (routes[:, 1:2] == expert_ids[None, :])
    index = jnp.arange(rows, dtype=jnp.int32)
    before = (index[:, None] > index[None, :]).astype(BF16)
    rank = jnp.dot(before, hit.astype(BF16), preferred_element_type=F32).astype(jnp.int32)
    slot_of = jnp.where(hit, rank, -1)
    slot_dup = jnp.repeat(slot_of.T, holders, axis=0)

    def pack(low):
        want = low + jnp.arange(slots, dtype=jnp.int32)
        return slot_dup[:, None, :] == want[None, :, None]

    picks = [pack(0), pack(slots)]

    def dispatch(pick):
        flat = pick.reshape(seq_count * slots, rows).astype(BF16)
        out = jnp.dot(flat, residual, preferred_element_type=F32).astype(BF16)
        got = lax.all_to_all(out.reshape(seq_count, slots, share), "seq", 0, 0, tiled=True)
        return got.reshape(seq_count * slots, share)

    gain_share = lax.dynamic_slice_in_dim(gain_moe, ten_rank * share, share)
    router = lax.dynamic_slice_in_dim(w_router, ten_rank * share, share)
    res32 = residual.astype(F32)
    part = jnp.dot(
        res32 * gain_share, router, preferred_element_type=F32, precision=lax.Precision.HIGHEST
    )
    square = jnp.sum(res32 * res32, axis=1, keepdims=True)
    stats = jnp.concatenate([part, square, jnp.zeros((rows, 7), F32)], axis=1)
    stats = stats + send_core(stats)
    stats = stats + lax.ppermute(stats, "tensor", [(t, t ^ 2) for t in range(ten_count)])
    stats = stats + lax.ppermute(stats, "tensor", [(t, t ^ 4) for t in range(ten_count)])
    logits = stats[:, :EXPERTS] * lax.rsqrt(stats[:, EXPERTS : EXPERTS + 1] / width + EPS)
    picked = routes[:, :, None] == expert_ids[None, None, :]
    chosen = jnp.sum(jnp.where(picked, logits[:, None, :], 0.0), axis=2)
    gates = jax.nn.softmax(chosen, axis=1)
    gate_of = jnp.sum(jnp.where(picked, gates[:, :, None], 0.0), axis=1)
    gate_dup = jnp.repeat(gate_of, holders, axis=1)

    gain_rows = gain_moe.reshape(ten_count, share)
    order = jnp.array([0, 3, 1, 2], jnp.int32)
    source = lax.rem(z + order, NZ) * 2
    ids = jnp.concatenate([source + c, source + other_c, out_ids])
    a_own = dispatch(picks[0])
    a_pieces = gather_ring(a_own)
    b_own = dispatch(picks[1])
    b_pieces = gather_ring(b_own)
    a_out = ffn(ids, gain_rows, w_gate, w_up, w_down, a_pieces, [b_own])
    a_sums, a_rest = scatter_start(*a_out)
    b_out = ffn(ids, gain_rows, w_gate, w_up, w_down, b_pieces, a_sums)
    b_sums, b_rest = scatter_start(*b_out)

    def give_back(parts):
        got = lax.all_to_all(parts.reshape(seq_count, slots, share), "seq", 0, 0, tiled=True)
        return got.reshape(seq_count * slots, share)

    a_final = scatter_end(a_sums, a_rest)
    b_final = scatter_end(b_sums, b_rest)
    a_back = give_back(a_final)
    b_back = give_back(b_final)

    def combine(pick, back):
        weight = jnp.where(pick.transpose(2, 0, 1), gate_dup[:, :, None], 0.0)
        weight = weight.reshape(rows, seq_count * slots)
        high = weight.astype(BF16)
        low = (weight - high.astype(F32)).astype(BF16)
        return jnp.dot(high, back, preferred_element_type=F32) + jnp.dot(
            low, back, preferred_element_type=F32
        )

    mixture = combine(picks[0], a_back) + combine(picks[1], b_back)
    layer_out = (res32 + mixture).astype(BF16)

    owner_ext = jnp.concatenate([owners, jnp.full((1,), -1, jnp.int32)])
    label_ids = jnp.arange(short_count + 2, dtype=jnp.int32)
    owner_tok = jnp.sum(
        jnp.where(labels[:, None] == label_ids[None, :], owner_ext[None, :], 0), axis=1
    )
    held = (owner_tok == seq_rank).reshape(seq_count, rows)
    held_b = held.astype(BF16)
    inside = jnp.dot(held_b, before.T, preferred_element_type=F32)
    seq_index = jnp.arange(seq_count, dtype=jnp.int32)
    earlier = (seq_index[:, None] > seq_index[None, :]).astype(BF16)
    sizes = jnp.sum(held.astype(F32), axis=1).astype(BF16)
    ahead = jnp.dot(earlier, sizes[:, None], preferred_element_type=F32)
    slot = jnp.where(held, (inside + ahead).astype(jnp.int32), -1).reshape(1, total)
    places = jnp.arange(total, dtype=jnp.int32)
    take = (places[:, None] == slot).astype(BF16)
    cache = jnp.dot(take, kv_all, preferred_element_type=F32)
    return layer_out, cache.astype(BF16)


def solution(mesh):
    return jax.shard_map(
        local,
        mesh=mesh,
        in_specs=(
            P("seq", None),
            P(),
            P("seq", None),
            P(),
            P(),
            P(None, "tensor"),
            P(None, "tensor"),
            P("tensor", None),
            P(),
            P(),
            P(None, ("seq", "tensor")),
            P(None, ("seq", "tensor")),
            P(("seq", "tensor"), None),
        ),
        out_specs=(P("seq", "tensor"), P("seq", "tensor")),
        check_vma=False,
    )
```

```python
import jax
import jax.numpy as jnp
from jax import lax
from jax.experimental import pallas as pl
from jax.experimental.pallas import tpu as pltpu
from jax.sharding import PartitionSpec as P


HEADS = 32
KV_HEADS = 8
HEAD_DIM = 128
EXPERTS = 8
EPS = 1e-05
THETA = 1000000.0
FLOOR = -1e30
NZ = 4
MIB = 1024 * 1024
F32 = jnp.float32
BF16 = jnp.bfloat16


VMEM_SPEC = pl.BlockSpec(memory_space=pltpu.VMEM)
ANY_SPEC = pl.BlockSpec(memory_space=pl.ANY)
HBM_SPEC = pl.BlockSpec(memory_space=pltpu.HBM)
SMEM_SPEC = pl.BlockSpec(memory_space=pltpu.SMEM)


def z_perm(step):
    return [(2 * z + c, 2 * ((z + step) % NZ) + c) for z in range(NZ) for c in range(2)]


def core_perm():
    return [(t, t ^ 1) for t in range(2 * NZ)]


def send_z(value, step):
    return lax.ppermute(value, "tensor", z_perm(step))


def send_core(value):
    return lax.ppermute(value, "tensor", core_perm())


def rotate(values, cosine, sine):
    half = values.shape[-1] // 2
    first = values[..., :half]
    second = values[..., half:]
    return jnp.concatenate(
        [first * cosine - second * sine, second * cosine + first * sine], axis=-1
    )


def attention_kernel(ids, first_ref, q_ref, start_ref, kv_ref, w_hbm, mine_ref, sib_ref, w_ref, sem):
    copy = pltpu.make_async_copy(w_hbm, w_ref, sem)
    copy.start()
    rows, dim = start_ref.shape[0], HEAD_DIM
    group = q_ref.shape[0] // rows
    count = kv_ref.shape[0]
    query = first_ref[0] + lax.broadcasted_iota(jnp.int32, (rows, count), 0)
    key = lax.broadcasted_iota(jnp.int32, (rows, count), 1)
    mask = (key <= query) & (key >= start_ref[...])
    scale = HEAD_DIM ** (-0.5)
    heads = []
    for g in range(group):
        q = q_ref[g * rows : (g + 1) * rows, :]
        s = lax.dot_general(
            q, kv_ref[:, :dim], (((1,), (1,)), ((), ())), preferred_element_type=F32
        )
        s = jnp.where(mask, s * scale, FLOOR)
        w = jnp.where(mask, jnp.exp(s - jnp.max(s, axis=1, keepdims=True)), 0.0)
        mass = jnp.sum(w, axis=1, keepdims=True)
        acc = jnp.dot(w.astype(BF16), kv_ref[:, dim:], preferred_element_type=F32)
        heads.append((acc / mass).astype(BF16))
    attended = jnp.concatenate(heads, axis=1)
    copy.wait()
    share = mine_ref.shape[2]

    def project(at):
        w = w_ref[:, pl.ds(pl.multiple_of(at * share, share), share)]
        return jnp.dot(attended, w, preferred_element_type=F32)

    def body(d, carry):
        sib_ref[d] = project(ids[4 + d]).astype(BF16)
        mine_ref[d] = project(ids[d])
        return carry

    lax.fori_loop(0, NZ, body, 0)


def attend(ids, first, q, start, kv, w_out, share):
    rows = start.shape[0]
    return pl.pallas_call(
        attention_kernel,
        out_shape=(
            jax.ShapeDtypeStruct((NZ, rows, share), F32),
            jax.ShapeDtypeStruct((NZ, rows, share), BF16),
        ),
        in_specs=[SMEM_SPEC, SMEM_SPEC, VMEM_SPEC, VMEM_SPEC, VMEM_SPEC, HBM_SPEC],
        out_specs=(VMEM_SPEC, VMEM_SPEC),
        scratch_shapes=[pltpu.VMEM(w_out.shape, BF16), pltpu.SemaphoreType.DMA],
        compiler_params=pltpu.CompilerParams(vmem_limit_bytes=24 * MIB),
    )(ids, first, q, start, kv, w_out)


def ffn_kernel(ids, gain_ref, wg_hbm, wu_hbm, wd_hbm, *refs):
    pieces = refs[:8]
    mine_ref, sib_ref = refs[-9:-7]
    xs_ref, act_ref, wg_ref, wu_ref, wd_ref, sems, _ = refs[-7:]
    copies = [
        pltpu.make_async_copy(hbm, ref, sems.at[i])
        for i, (hbm, ref) in enumerate(((wg_hbm, wg_ref), (wu_hbm, wu_ref), (wd_hbm, wd_ref)))
    ]
    for copy in copies:
        copy.start()
    rows, share = pieces[0].shape
    width = wg_ref.shape[0]
    tile = 32

    def norm(i, carry):
        at_row = pl.ds(pl.multiple_of(i * tile, tile), tile)
        total = jnp.zeros((tile, share), F32)
        for ref in pieces:
            v = ref[at_row, :].astype(F32)
            total = total + v * v
        mean = jnp.sum(total, axis=1, keepdims=True) * (1.0 / width)
        scale = lax.rsqrt(mean + EPS)
        for k, ref in enumerate(pieces):
            at = ids[k]
            v = ref[at_row, :].astype(F32) * scale * gain_ref[pl.ds(at, 1), :]
            xs_ref[at_row, pl.ds(pl.multiple_of(at * share, share), share)] = v.astype(BF16)
        return carry

    lax.fori_loop(0, rows // tile, norm, 0)
    copies[0].wait()
    copies[1].wait()
    block = 256

    def hidden(i, carry):
        at_row = pl.ds(pl.multiple_of(i * block, block), block)
        v = xs_ref[at_row, :]
        gate = jnp.dot(v, wg_ref[...], preferred_element_type=F32)
        up = jnp.dot(v, wu_ref[...], preferred_element_type=F32)
        act_ref[at_row, :] = (gate / (1.0 + jnp.exp(-gate)) * up).astype(BF16)
        return carry

    lax.fori_loop(0, rows // block, hidden, 0)
    copies[2].wait()

    def down(at):
        w = wd_ref[:, pl.ds(pl.multiple_of(at * share, share), share)]
        return jnp.dot(act_ref[...], w, preferred_element_type=F32).astype(BF16)

    def body(d, carry):
        sib_ref[d] = down(ids[12 + d])
        mine_ref[d] = down(ids[8 + d])
        return carry

    lax.fori_loop(0, NZ, body, 0)


def ffn(ids, gain, w_gate, w_up, w_down, pieces, after):
    rows, share = pieces[0].shape
    return pl.pallas_call(
        ffn_kernel,
        out_shape=(
            jax.ShapeDtypeStruct((NZ, rows, share), BF16),
            jax.ShapeDtypeStruct((NZ, rows, share), BF16),
        ),
        in_specs=[SMEM_SPEC, VMEM_SPEC]
        + [HBM_SPEC] * 3
        + [VMEM_SPEC] * len(pieces)
        + [ANY_SPEC] * len(after),
        out_specs=(VMEM_SPEC,) * 2,
        scratch_shapes=[
            pltpu.VMEM((rows, w_gate.shape[0]), BF16),
            pltpu.VMEM((rows, w_gate.shape[1]), BF16),
            pltpu.VMEM(w_gate.shape, BF16),
            pltpu.VMEM(w_up.shape, BF16),
            pltpu.VMEM(w_down.shape, BF16),
            pltpu.SemaphoreType.DMA((3,)),
            pltpu.VMEM((8, 128), F32),
        ],
        compiler_params=pltpu.CompilerParams(vmem_limit_bytes=36 * MIB),
    )(ids, gain, w_gate, w_up, w_down, *pieces, *after)


def gather_ring(own):
    ring = [own] + [send_z(own, d) for d in (1, 3, 2)]
    near = [send_core(own)]
    return ring + near + [send_core(v) for v in ring[1:]]


def add(*parts):
    total = parts[0].astype(F32)
    for part in parts[1:]:
        total = total + part.astype(F32)
    return total.astype(BF16)


def scatter_start(mine, sib):
    got = send_core(sib)
    return [add(mine[d], got[d]) for d in range(1, NZ)], (mine[0], got[0])


def scatter_end(sums, own):
    moved = [send_z(sums[d - 1], d) for d in (1, 3, 2)]
    return add(*own, *moved)


def local(
    tokens,
    segment_ids,
    routes,
    owners,
    gain_attn,
    w_query,
    w_kv,
    w_out,
    gain_moe,
    w_router,
    w_gate,
    w_up,
    w_down,
):
    seq_count = lax.axis_size("seq")
    ten_count = lax.axis_size("tensor")
    seq_rank = lax.axis_index("seq").astype(jnp.int32)
    ten_rank = lax.axis_index("tensor").astype(jnp.int32)
    rows, width = tokens.shape
    total = segment_ids.shape[0]
    w_out, w_gate, w_up, w_down = (
        pltpu.with_memory_space_constraint(w, pltpu.HBM) for w in (w_out, w_gate, w_up, w_down)
    )
    share = width // ten_count
    group = HEADS // KV_HEADS
    z = ten_rank // 2
    c = ten_rank - z * 2
    first = seq_rank * rows

    short_count = owners.shape[0] - 1
    labels = jnp.where(segment_ids < 0, short_count + 1, segment_ids)
    my_labels = lax.dynamic_slice_in_dim(labels, first, rows)
    seg_start = jnp.sum((labels[None, :] < my_labels[:, None]).astype(jnp.int32), axis=1)
    position = first + jnp.arange(rows, dtype=jnp.int32) - seg_start

    values = tokens.astype(F32)
    scale = lax.rsqrt(jnp.mean(values * values, axis=-1, keepdims=True) + EPS)
    normed = (values * scale * gain_attn).astype(BF16)
    half_dim = HEAD_DIM // 2
    freqs = THETA ** (-(jnp.arange(half_dim, dtype=F32) * 2.0) / HEAD_DIM)
    angles = position.astype(F32)[:, None] * freqs[None, :]
    cosine = jnp.cos(angles)
    sine = jnp.sin(angles)
    pairs = jnp.dot(normed, w_kv, preferred_element_type=F32)
    keys = rotate(pairs[:, :HEAD_DIM], cosine, sine).astype(BF16)
    kv_own = jnp.concatenate([keys, pairs[:, HEAD_DIM:].astype(BF16)], axis=1)
    queries = jnp.dot(normed, w_query, preferred_element_type=F32)
    q = jnp.concatenate(
        [
            rotate(queries[:, g * HEAD_DIM : (g + 1) * HEAD_DIM], cosine, sine).astype(BF16)
            for g in range(group)
        ],
        axis=0,
    )

    kv_all = lax.all_to_all(
        jnp.broadcast_to(kv_own[None], (seq_count,) + kv_own.shape), "seq", 0, 0, tiled=True
    ).reshape(total, kv_own.shape[1])

    ring = lax.rem(z + jnp.arange(NZ, dtype=jnp.int32), NZ) * 2
    other_c = 1 - c
    out_ids = jnp.concatenate([ring + c, ring + other_c])
    out_mine, out_sib = attend(
        out_ids, first.reshape(1), q, seg_start[:, None], kv_all, w_out, share
    )
    out_sib_r = send_core(out_sib)
    sums = [out_mine[d] + out_sib_r[d].astype(F32) for d in range(NZ)]
    attn_sum = sums[0]
    for d in (1, 3, 2):
        attn_sum = attn_sum + send_z(sums[d].astype(BF16), d).astype(F32)
    own_tokens = lax.dynamic_slice_in_dim(tokens, ten_rank * share, share, 1)
    residual = (own_tokens.astype(F32) + attn_sum).astype(BF16)

    capacity = rows // 2
    slots = capacity // 2
    holders = seq_count // EXPERTS
    expert_ids = jnp.arange(EXPERTS, dtype=jnp.int32)
    hit = (routes[:, 0:1] == expert_ids[None, :]) | (routes[:, 1:2] == expert_ids[None, :])
    index = jnp.arange(rows, dtype=jnp.int32)
    before = (index[:, None] > index[None, :]).astype(BF16)
    rank = jnp.dot(before, hit.astype(BF16), preferred_element_type=F32).astype(jnp.int32)
    slot_of = jnp.where(hit, rank, -1)
    slot_dup = jnp.repeat(slot_of.T, holders, axis=0)

    def pack(low):
        want = low + jnp.arange(slots, dtype=jnp.int32)
        return slot_dup[:, None, :] == want[None, :, None]

    picks = [pack(0), pack(slots)]

    def dispatch(pick):
        flat = pick.reshape(seq_count * slots, rows).astype(BF16)
        out = jnp.dot(flat, residual, preferred_element_type=F32).astype(BF16)
        got = lax.all_to_all(out.reshape(seq_count, slots, share), "seq", 0, 0, tiled=True)
        return got.reshape(seq_count * slots, share)

    gain_share = lax.dynamic_slice_in_dim(gain_moe, ten_rank * share, share)
    router = lax.dynamic_slice_in_dim(w_router, ten_rank * share, share)
    res32 = residual.astype(F32)
    part = jnp.dot(
        res32 * gain_share, router, preferred_element_type=F32, precision=lax.Precision.HIGHEST
    )
    square = jnp.sum(res32 * res32, axis=1, keepdims=True)
    stats = jnp.concatenate([part, square, jnp.zeros((rows, 7), F32)], axis=1)
    stats = stats + send_core(stats)
    stats = stats + lax.ppermute(stats, "tensor", [(t, t ^ 2) for t in range(ten_count)])
    stats = stats + lax.ppermute(stats, "tensor", [(t, t ^ 4) for t in range(ten_count)])
    logits = stats[:, :EXPERTS] * lax.rsqrt(stats[:, EXPERTS : EXPERTS + 1] / width + EPS)
    picked = routes[:, :, None] == expert_ids[None, None, :]
    chosen = jnp.sum(jnp.where(picked, logits[:, None, :], 0.0), axis=2)
    gates = jax.nn.softmax(chosen, axis=1)
    gate_of = jnp.sum(jnp.where(picked, gates[:, :, None], 0.0), axis=1)
    gate_dup = jnp.repeat(gate_of, holders, axis=1)

    gain_rows = gain_moe.reshape(ten_count, share)
    order = jnp.array([0, 3, 1, 2], jnp.int32)
    source = lax.rem(z + order, NZ) * 2
    ids = jnp.concatenate([source + c, source + other_c, out_ids])
    a_own = dispatch(picks[0])
    a_pieces = gather_ring(a_own)
    b_own = dispatch(picks[1])
    b_pieces = gather_ring(b_own)
    a_out = ffn(ids, gain_rows, w_gate, w_up, w_down, a_pieces, [b_own])
    a_sums, a_rest = scatter_start(*a_out)
    b_out = ffn(ids, gain_rows, w_gate, w_up, w_down, b_pieces, a_sums)
    b_sums, b_rest = scatter_start(*b_out)

    def give_back(parts):
        got = lax.all_to_all(parts.reshape(seq_count, slots, share), "seq", 0, 0, tiled=True)
        return got.reshape(seq_count * slots, share)

    a_final = scatter_end(a_sums, a_rest)
    b_final = scatter_end(b_sums, b_rest)
    a_back = give_back(a_final)
    b_back = give_back(b_final)

    def combine(pick, back):
        weight = jnp.where(pick.transpose(2, 0, 1), gate_dup[:, :, None], 0.0)
        weight = weight.reshape(rows, seq_count * slots)
        high = weight.astype(BF16)
        low = (weight - high.astype(F32)).astype(BF16)
        return jnp.dot(high, back, preferred_element_type=F32) + jnp.dot(
            low, back, preferred_element_type=F32
        )

    mixture = combine(picks[0], a_back) + combine(picks[1], b_back)
    layer_out = (res32 + mixture).astype(BF16)

    owner_ext = jnp.concatenate([owners, jnp.full((1,), -1, jnp.int32)])
    label_ids = jnp.arange(short_count + 2, dtype=jnp.int32)
    owner_tok = jnp.sum(
        jnp.where(labels[:, None] == label_ids[None, :], owner_ext[None, :], 0), axis=1
    )
    held = (owner_tok == seq_rank).reshape(seq_count, rows)
    held_b = held.astype(BF16)
    inside = jnp.dot(held_b, before.T, preferred_element_type=F32)
    seq_index = jnp.arange(seq_count, dtype=jnp.int32)
    earlier = (seq_index[:, None] > seq_index[None, :]).astype(BF16)
    sizes = jnp.sum(held.astype(F32), axis=1).astype(BF16)
    ahead = jnp.dot(earlier, sizes[:, None], preferred_element_type=F32)
    slot = jnp.where(held, (inside + ahead).astype(jnp.int32), -1).reshape(1, total)
    places = jnp.arange(total, dtype=jnp.int32)
    take = (places[:, None] == slot).astype(BF16)
    cache = jnp.dot(take, kv_all, preferred_element_type=F32)
    return layer_out, cache.astype(BF16)


def solution(mesh):
    return jax.shard_map(
        local,
        mesh=mesh,
        in_specs=(
            P("seq", None),
            P(),
            P("seq", None),
            P(),
            P(),
            P(None, "tensor"),
            P(None, "tensor"),
            P("tensor", None),
            P(),
            P(),
            P(None, ("seq", "tensor")),
            P(None, ("seq", "tensor")),
            P(("seq", "tensor"), None),
        ),
        out_specs=(P("seq", "tensor"), P("seq", "tensor")),
        check_vma=False,
    )
```

```python
import jax
import jax.numpy as jnp
from jax import lax
from jax.experimental import pallas as pl
from jax.experimental.pallas import tpu as pltpu
from jax.sharding import PartitionSpec as P


HEADS = 32
KV_HEADS = 8
HEAD_DIM = 128
EXPERTS = 8
EPS = 1e-05
THETA = 1000000.0
FLOOR = -1e30
NZ = 4
MIB = 1024 * 1024
F32 = jnp.float32
BF16 = jnp.bfloat16


VMEM_SPEC = pl.BlockSpec(memory_space=pltpu.VMEM)
ANY_SPEC = pl.BlockSpec(memory_space=pl.ANY)
HBM_SPEC = pl.BlockSpec(memory_space=pltpu.HBM)
SMEM_SPEC = pl.BlockSpec(memory_space=pltpu.SMEM)


def z_perm(step):
    return [(2 * z + c, 2 * ((z + step) % NZ) + c) for z in range(NZ) for c in range(2)]


def core_perm():
    return [(t, t ^ 1) for t in range(2 * NZ)]


def send_z(value, step):
    return lax.ppermute(value, "tensor", z_perm(step))


def send_core(value):
    return lax.ppermute(value, "tensor", core_perm())


def rotate(values, cosine, sine):
    half = values.shape[-1] // 2
    first = values[..., :half]
    second = values[..., half:]
    return jnp.concatenate(
        [first * cosine - second * sine, second * cosine + first * sine], axis=-1
    )


def attention_kernel(ids, first_ref, q_ref, start_ref, kv_ref, w_hbm, mine_ref, sib_ref, w_ref, sem):
    copy = pltpu.make_async_copy(w_hbm, w_ref, sem)
    copy.start()
    rows, dim = start_ref.shape[0], HEAD_DIM
    group = q_ref.shape[0] // rows
    count = kv_ref.shape[0]
    query = first_ref[0] + lax.broadcasted_iota(jnp.int32, (rows, count), 0)
    key = lax.broadcasted_iota(jnp.int32, (rows, count), 1)
    mask = (key <= query) & (key >= start_ref[...])
    scale = HEAD_DIM ** (-0.5)
    heads = []
    for g in range(group):
        q = q_ref[g * rows : (g + 1) * rows, :]
        s = lax.dot_general(
            q, kv_ref[:, :dim], (((1,), (1,)), ((), ())), preferred_element_type=F32
        )
        s = jnp.where(mask, s * scale, FLOOR)
        w = jnp.exp(s - jnp.max(s, axis=1, keepdims=True))
        mass = jnp.sum(w, axis=1, keepdims=True)
        acc = jnp.dot(w.astype(BF16), kv_ref[:, dim:], preferred_element_type=F32)
        heads.append((acc / mass).astype(BF16))
    attended = jnp.concatenate(heads, axis=1)
    copy.wait()
    share = mine_ref.shape[2]

    def project(at):
        w = w_ref[:, pl.ds(pl.multiple_of(at * share, share), share)]
        return jnp.dot(attended, w, preferred_element_type=F32)

    def body(d, carry):
        sib_ref[d] = project(ids[4 + d]).astype(BF16)
        mine_ref[d] = project(ids[d])
        return carry

    lax.fori_loop(0, NZ, body, 0)


def attend(ids, first, q, start, kv, w_out, share):
    rows = start.shape[0]
    return pl.pallas_call(
        attention_kernel,
        out_shape=(
            jax.ShapeDtypeStruct((NZ, rows, share), F32),
            jax.ShapeDtypeStruct((NZ, rows, share), BF16),
        ),
        in_specs=[SMEM_SPEC, SMEM_SPEC, VMEM_SPEC, VMEM_SPEC, VMEM_SPEC, HBM_SPEC],
        out_specs=(VMEM_SPEC, VMEM_SPEC),
        scratch_shapes=[pltpu.VMEM(w_out.shape, BF16), pltpu.SemaphoreType.DMA],
        compiler_params=pltpu.CompilerParams(vmem_limit_bytes=24 * MIB),
    )(ids, first, q, start, kv, w_out)


def ffn_kernel(ids, gain_ref, wg_hbm, wu_hbm, wd_hbm, *refs):
    pieces = refs[:10]
    mine_ref, sib_ref = refs[-8:-6]
    xs_ref, act_ref, wg_ref, wu_ref, wd_ref, sems = refs[-6:]
    copies = [
        pltpu.make_async_copy(hbm, ref, sems.at[i])
        for i, (hbm, ref) in enumerate(((wg_hbm, wg_ref), (wu_hbm, wu_ref), (wd_hbm, wd_ref)))
    ]
    for copy in copies:
        copy.start()
    rows, share = pieces[0].shape
    half = rows // 2
    width = wg_ref.shape[0]
    tile = 32

    for side in range(2):
        chosen = [(pieces[5 * s + k], 0, 4 * s + k) for s in range(2) for k in range(3)]
        chosen += [(pieces[5 * s + 3 + side], side * half, 4 * s + 3) for s in range(2)]

        def norm(i, carry):
            at_row = pl.multiple_of(side * half + i * tile, tile)
            total = jnp.zeros((tile, share), F32)
            for ref, low, _ in chosen:
                v = ref[pl.ds(pl.multiple_of(at_row - low, tile), tile), :].astype(F32)
                total = total + v * v
            mean = jnp.sum(total, axis=1, keepdims=True) * (1.0 / width)
            scale = lax.rsqrt(mean + EPS)
            for ref, low, k in chosen:
                at = ids[k]
                v = ref[pl.ds(pl.multiple_of(at_row - low, tile), tile), :].astype(F32)
                v = v * scale * gain_ref[pl.ds(at, 1), :]
                column = pl.ds(pl.multiple_of(at * share, share), share)
                xs_ref[pl.ds(at_row, tile), column] = v.astype(BF16)
            return carry

        lax.fori_loop(0, half // tile, norm, 0)
    copies[0].wait()
    copies[1].wait()

    def hidden(i, carry):
        at_row = pl.ds(pl.multiple_of(i * half, half), half)
        v = xs_ref[at_row, :]
        gate = jnp.dot(v, wg_ref[...], preferred_element_type=F32)
        up = jnp.dot(v, wu_ref[...], preferred_element_type=F32)
        act_ref[at_row, :] = (gate / (1.0 + jnp.exp(-gate)) * up).astype(BF16)
        return carry

    lax.fori_loop(0, 2, hidden, 0)
    copies[2].wait()

    def body(i, carry):
        block = i // 2
        at_row = pl.ds(pl.multiple_of((i - block * 2) * half, half), half)
        for ref, base in ((sib_ref, 16), (mine_ref, 8)):
            w = wd_ref[:, pl.ds(pl.multiple_of(ids[base + i] * share, share), share)]
            out = jnp.dot(act_ref[at_row, :], w, preferred_element_type=F32)
            ref[block, at_row, :] = out.astype(BF16)
        return carry

    lax.fori_loop(0, 8, body, 0)


def ffn(ids, gain, w_gate, w_up, w_down, pieces, after):
    rows, share = pieces[0].shape
    return pl.pallas_call(
        ffn_kernel,
        out_shape=(
            jax.ShapeDtypeStruct((NZ, rows, share), BF16),
            jax.ShapeDtypeStruct((NZ, rows, share), BF16),
        ),
        in_specs=[SMEM_SPEC, VMEM_SPEC]
        + [HBM_SPEC] * 3
        + [VMEM_SPEC] * len(pieces)
        + [ANY_SPEC] * len(after),
        out_specs=(VMEM_SPEC,) * 2,
        scratch_shapes=[
            pltpu.VMEM((rows, w_gate.shape[0]), BF16),
            pltpu.VMEM((rows, w_gate.shape[1]), BF16),
            pltpu.VMEM(w_gate.shape, BF16),
            pltpu.VMEM(w_up.shape, BF16),
            pltpu.VMEM(w_down.shape, BF16),
            pltpu.SemaphoreType.DMA((3,)),
        ],
        compiler_params=pltpu.CompilerParams(vmem_limit_bytes=36 * MIB),
    )(ids, gain, w_gate, w_up, w_down, *pieces, *after)


def gather_ring(own):
    half = own.shape[0] // 2
    below = send_z(own, 1)
    above = send_z(own, -1)
    far_a = send_z(below[:half], 1)
    far_b = send_z(above[half:], -1)
    own_s = send_core(own)
    near_s = [send_core(below), send_core(above)]
    far_s = [send_core(far_a), send_core(far_b)]
    return [own, below, above, far_a, far_b, own_s] + near_s + far_s


def mix_kernel(mine_ref, got_ref, up_ref, down_ref):
    for k, ref in enumerate((up_ref, down_ref)):
        ref[...] = (mine_ref[k].astype(F32) + got_ref[k].astype(F32)).astype(BF16)


def relay_kernel(mine_ref, got_ref, below_ref, above_ref, low_ref, high_ref):
    total = mine_ref[0].astype(F32) + got_ref[0].astype(F32)
    half = low_ref.shape[0]
    low_ref[...] = (total[:half] + below_ref[:half, :].astype(F32)).astype(BF16)
    high_ref[...] = (total[half:] + above_ref[half:, :].astype(F32)).astype(BF16)


def end_kernel(mine_ref, got_ref, below_ref, above_ref, low_ref, high_ref, out_ref):
    total = mine_ref[0].astype(F32) + got_ref[0].astype(F32)
    half = low_ref.shape[0]
    first = total[:half] + above_ref[:half, :].astype(F32) + low_ref[...].astype(F32)
    second = total[half:] + below_ref[half:, :].astype(F32) + high_ref[...].astype(F32)
    out_ref[:half, :] = first.astype(BF16)
    out_ref[half:, :] = second.astype(BF16)


def combine_blocks(kernel, pair, count, index, more, outs):
    _, rows, share = pair[0].shape
    block = pl.BlockSpec((count, rows, share), lambda i: (index, 0, 0))

    def whole(height):
        return pl.BlockSpec((height, share), lambda i: (0, 0))

    return pl.pallas_call(
        kernel,
        grid=(1,),
        out_shape=tuple(jax.ShapeDtypeStruct((height, share), BF16) for height in outs),
        in_specs=[block, block] + [whole(v.shape[0]) for v in more],
        out_specs=tuple(whole(height) for height in outs),
        compiler_params=pltpu.CompilerParams(vmem_limit_bytes=16 * MIB),
    )(*pair, *more)


def scatter_start(mine, sib):
    rows = mine.shape[1]
    got = send_core(sib)
    return *combine_blocks(mix_kernel, (mine, got), 2, 0, (), (rows, rows)), mine, got


def scatter_end(up, down, mine, got):
    rows = up.shape[0]
    half = rows // 2
    from_below = send_z(up, 1)
    from_above = send_z(down, -1)
    moved = (from_below, from_above)
    low, high = combine_blocks(relay_kernel, (mine, got), 1, 2, moved, (half, half))
    last = (send_z(low, 1), send_z(high, -1))
    return combine_blocks(end_kernel, (mine, got), 1, 3, moved + last, (rows,))[0]


def local(
    tokens,
    segment_ids,
    routes,
    owners,
    gain_attn,
    w_query,
    w_kv,
    w_out,
    gain_moe,
    w_router,
    w_gate,
    w_up,
    w_down,
):
    seq_count = lax.axis_size("seq")
    ten_count = lax.axis_size("tensor")
    seq_rank = lax.axis_index("seq").astype(jnp.int32)
    ten_rank = lax.axis_index("tensor").astype(jnp.int32)
    rows, width = tokens.shape
    total = segment_ids.shape[0]
    w_out, w_gate, w_up, w_down = (
        pltpu.with_memory_space_constraint(w, pltpu.HBM) for w in (w_out, w_gate, w_up, w_down)
    )
    share = width // ten_count
    group = HEADS // KV_HEADS
    z = ten_rank // 2
    c = ten_rank - z * 2
    first = seq_rank * rows

    short_count = owners.shape[0] - 1
    labels = jnp.where(segment_ids < 0, short_count + 1, segment_ids)
    my_labels = lax.dynamic_slice_in_dim(labels, first, rows)
    seg_start = jnp.sum((labels[None, :] < my_labels[:, None]).astype(jnp.int32), axis=1)
    position = first + jnp.arange(rows, dtype=jnp.int32) - seg_start

    values = tokens.astype(F32)
    scale = lax.rsqrt(jnp.mean(values * values, axis=-1, keepdims=True) + EPS)
    normed = (values * scale * gain_attn).astype(BF16)
    half_dim = HEAD_DIM // 2
    freqs = THETA ** (-(jnp.arange(half_dim, dtype=F32) * 2.0) / HEAD_DIM)
    angles = position.astype(F32)[:, None] * freqs[None, :]
    cosine = jnp.cos(angles)
    sine = jnp.sin(angles)
    pairs = jnp.dot(normed, w_kv, preferred_element_type=F32)
    keys = rotate(pairs[:, :HEAD_DIM], cosine, sine).astype(BF16)
    kv_own = jnp.concatenate([keys, pairs[:, HEAD_DIM:].astype(BF16)], axis=1)
    queries = jnp.dot(normed, w_query, preferred_element_type=F32)
    q = jnp.concatenate(
        [
            rotate(queries[:, g * HEAD_DIM : (g + 1) * HEAD_DIM], cosine, sine).astype(BF16)
            for g in range(group)
        ],
        axis=0,
    )

    kv_all = lax.all_to_all(
        jnp.broadcast_to(kv_own[None], (seq_count,) + kv_own.shape), "seq", 0, 0, tiled=True
    ).reshape(total, kv_own.shape[1])

    ring = lax.rem(z + jnp.arange(NZ, dtype=jnp.int32), NZ) * 2
    other_c = 1 - c
    out_ids = jnp.concatenate([ring + c, ring + other_c])
    out_mine, out_sib = attend(
        out_ids, first.reshape(1), q, seg_start[:, None], kv_all, w_out, share
    )
    out_sib_r = send_core(out_sib)
    sums = [out_mine[d] + out_sib_r[d].astype(F32) for d in range(NZ)]
    attn_sum = sums[0]
    for d in (1, 3, 2):
        attn_sum = attn_sum + send_z(sums[d].astype(BF16), d).astype(F32)
    own_tokens = lax.dynamic_slice_in_dim(tokens, ten_rank * share, share, 1)
    residual = (own_tokens.astype(F32) + attn_sum).astype(BF16)

    capacity = rows // 2
    slots = capacity // 2
    holders = seq_count // EXPERTS
    expert_ids = jnp.arange(EXPERTS, dtype=jnp.int32)
    hit = (routes[:, 0:1] == expert_ids[None, :]) | (routes[:, 1:2] == expert_ids[None, :])
    index = jnp.arange(rows, dtype=jnp.int32)
    before = (index[:, None] > index[None, :]).astype(BF16)
    rank = jnp.dot(before, hit.astype(BF16), preferred_element_type=F32).astype(jnp.int32)
    slot_of = jnp.where(hit, rank, -1)
    slot_dup = jnp.repeat(slot_of.T, holders, axis=0)

    def pack(low):
        want = low + jnp.arange(slots, dtype=jnp.int32)
        return slot_dup[:, None, :] == want[None, :, None]

    picks = [pack(0), pack(slots)]

    def dispatch(pick):
        flat = pick.reshape(seq_count * slots, rows).astype(BF16)
        out = jnp.dot(flat, residual, preferred_element_type=F32).astype(BF16)
        got = lax.all_to_all(out.reshape(seq_count, slots, share), "seq", 0, 0, tiled=True)
        return got.reshape(seq_count * slots, share)

    gain_share = lax.dynamic_slice_in_dim(gain_moe, ten_rank * share, share)
    router = lax.dynamic_slice_in_dim(w_router, ten_rank * share, share)
    res32 = residual.astype(F32)
    part = jnp.dot(
        res32 * gain_share, router, preferred_element_type=F32, precision=lax.Precision.HIGHEST
    )
    square = jnp.sum(res32 * res32, axis=1, keepdims=True)
    stats = jnp.concatenate([part, square, jnp.zeros((rows, 7), F32)], axis=1)
    stats = stats + send_core(stats)
    stats = stats + lax.ppermute(stats, "tensor", [(t, t ^ 2) for t in range(ten_count)])
    stats = stats + lax.ppermute(stats, "tensor", [(t, t ^ 4) for t in range(ten_count)])
    logits = stats[:, :EXPERTS] * lax.rsqrt(stats[:, EXPERTS : EXPERTS + 1] / width + EPS)
    picked = routes[:, :, None] == expert_ids[None, None, :]
    chosen = jnp.sum(jnp.where(picked, logits[:, None, :], 0.0), axis=2)
    gates = jax.nn.softmax(chosen, axis=1)
    gate_of = jnp.sum(jnp.where(picked, gates[:, :, None], 0.0), axis=1)
    gate_dup = jnp.repeat(gate_of, holders, axis=1)

    gain_rows = gain_moe.reshape(ten_count, share)
    source = lax.rem(z + jnp.array([0, 3, 1, 2], jnp.int32), NZ) * 2
    target = lax.rem(z + jnp.array([2, 1, 3, 2, 1, 3, 0, 0], jnp.int32), NZ) * 2
    ids = jnp.concatenate([source + c, source + other_c, target + c, target + other_c])
    a_own = dispatch(picks[0])
    a_pieces = gather_ring(a_own)
    b_own = dispatch(picks[1])
    b_pieces = gather_ring(b_own)
    a_out = ffn(ids, gain_rows, w_gate, w_up, w_down, a_pieces, [])
    a_start = scatter_start(*a_out)
    b_out = ffn(ids, gain_rows, w_gate, w_up, w_down, b_pieces, a_start[:2])
    b_start = scatter_start(*b_out)

    def give_back(parts):
        got = lax.all_to_all(parts.reshape(seq_count, slots, share), "seq", 0, 0, tiled=True)
        return got.reshape(seq_count * slots, share)

    a_final = scatter_end(*a_start)
    b_final = scatter_end(*b_start)
    a_back = give_back(a_final)
    b_back = give_back(b_final)

    def combine(pick, back):
        weight = jnp.where(pick.transpose(2, 0, 1), gate_dup[:, :, None], 0.0)
        weight = weight.reshape(rows, seq_count * slots)
        high = weight.astype(BF16)
        low = (weight - high.astype(F32)).astype(BF16)
        return jnp.dot(high, back, preferred_element_type=F32) + jnp.dot(
            low, back, preferred_element_type=F32
        )

    mixture = combine(picks[0], a_back) + combine(picks[1], b_back)
    layer_out = (res32 + mixture).astype(BF16)

    owner_ext = jnp.concatenate([owners, jnp.full((1,), -1, jnp.int32)])
    label_ids = jnp.arange(short_count + 2, dtype=jnp.int32)
    owner_tok = jnp.sum(
        jnp.where(labels[:, None] == label_ids[None, :], owner_ext[None, :], 0), axis=1
    )
    held = (owner_tok == seq_rank).reshape(seq_count, rows)
    held_b = held.astype(BF16)
    inside = jnp.dot(held_b, before.T, preferred_element_type=F32)
    seq_index = jnp.arange(seq_count, dtype=jnp.int32)
    earlier = (seq_index[:, None] > seq_index[None, :]).astype(BF16)
    sizes = jnp.sum(held.astype(F32), axis=1).astype(BF16)
    ahead = jnp.dot(earlier, sizes[:, None], preferred_element_type=F32)
    slot = jnp.where(held, (inside + ahead).astype(jnp.int32), -1).reshape(1, total)
    places = jnp.arange(total, dtype=jnp.int32)
    take = (places[:, None] == slot).astype(BF16)
    cache = jnp.dot(take, kv_all, preferred_element_type=F32)
    return layer_out, cache.astype(BF16)


def solution(mesh):
    return jax.shard_map(
        local,
        mesh=mesh,
        in_specs=(
            P("seq", None),
            P(),
            P("seq", None),
            P(),
            P(),
            P(None, "tensor"),
            P(None, "tensor"),
            P("tensor", None),
            P(),
            P(),
            P(None, ("seq", "tensor")),
            P(None, ("seq", "tensor")),
            P(("seq", "tensor"), None),
        ),
        out_specs=(P("seq", "tensor"), P("seq", "tensor")),
        check_vma=False,
    )
```

```python
import jax
import jax.numpy as jnp
from jax import lax
from jax.experimental import pallas as pl
from jax.experimental.pallas import tpu as pltpu
from jax.sharding import PartitionSpec as P


HEADS = 32
KV_HEADS = 8
HEAD_DIM = 128
EXPERTS = 8
EPS = 1e-05
THETA = 1000000.0
FLOOR = -1e30
NZ = 4
MIB = 1024 * 1024
F32 = jnp.float32
BF16 = jnp.bfloat16


VMEM_SPEC = pl.BlockSpec(memory_space=pltpu.VMEM)
ANY_SPEC = pl.BlockSpec(memory_space=pl.ANY)
HBM_SPEC = pl.BlockSpec(memory_space=pltpu.HBM)
SMEM_SPEC = pl.BlockSpec(memory_space=pltpu.SMEM)


def z_perm(step):
    return [(2 * z + c, 2 * ((z + step) % NZ) + c) for z in range(NZ) for c in range(2)]


def core_perm():
    return [(t, t ^ 1) for t in range(2 * NZ)]


def send_z(value, step):
    return lax.ppermute(value, "tensor", z_perm(step))


def send_core(value):
    return lax.ppermute(value, "tensor", core_perm())


def rotate(values, cosine, sine):
    half = values.shape[-1] // 2
    first = values[..., :half]
    second = values[..., half:]
    return jnp.concatenate(
        [first * cosine - second * sine, second * cosine + first * sine], axis=-1
    )


def attention_kernel(ids, first_ref, q_ref, start_ref, kv_ref, w_hbm, mine_ref, sib_ref, w_ref, sem):
    copy = pltpu.make_async_copy(w_hbm, w_ref, sem)
    copy.start()
    rows, dim = start_ref.shape[0], HEAD_DIM
    group = q_ref.shape[0] // rows
    count = kv_ref.shape[0]
    query = first_ref[0] + lax.broadcasted_iota(jnp.int32, (rows, count), 0)
    key = lax.broadcasted_iota(jnp.int32, (rows, count), 1)
    mask = (key <= query) & (key >= start_ref[...])
    scale = HEAD_DIM ** (-0.5)
    heads = []
    for g in range(group):
        q = q_ref[g * rows : (g + 1) * rows, :]
        s = lax.dot_general(
            q, kv_ref[:, :dim], (((1,), (1,)), ((), ())), preferred_element_type=F32
        )
        s = jnp.where(mask, s * scale, FLOOR)
        w = jnp.exp(s - jnp.max(s, axis=1, keepdims=True))
        mass = jnp.sum(w, axis=1, keepdims=True)
        acc = jnp.dot(w.astype(BF16), kv_ref[:, dim:], preferred_element_type=F32)
        heads.append((acc / mass).astype(BF16))
    attended = jnp.concatenate(heads, axis=1)
    copy.wait()
    share = mine_ref.shape[2]

    def project(at):
        w = w_ref[:, pl.ds(pl.multiple_of(at * share, share), share)]
        return jnp.dot(attended, w, preferred_element_type=F32)

    def body(d, carry):
        sib_ref[d] = project(ids[4 + d]).astype(BF16)
        mine_ref[d] = project(ids[d])
        return carry

    lax.fori_loop(0, NZ, body, 0)


def attend(ids, first, q, start, kv, w_out, share):
    rows = start.shape[0]
    return pl.pallas_call(
        attention_kernel,
        out_shape=(
            jax.ShapeDtypeStruct((NZ, rows, share), F32),
            jax.ShapeDtypeStruct((NZ, rows, share), BF16),
        ),
        in_specs=[SMEM_SPEC, SMEM_SPEC, VMEM_SPEC, VMEM_SPEC, VMEM_SPEC, HBM_SPEC],
        out_specs=(VMEM_SPEC, VMEM_SPEC),
        scratch_shapes=[pltpu.VMEM(w_out.shape, BF16), pltpu.SemaphoreType.DMA],
        compiler_params=pltpu.CompilerParams(vmem_limit_bytes=24 * MIB),
    )(ids, first, q, start, kv, w_out)


def ffn_kernel(ids, gain_ref, *refs):
    weights = refs[:6]
    pieces = refs[6:11]
    outs = refs[-10:-6]
    xs_ref, act_ref, gate_ref, up_ref, down_ref, sems = refs[-6:]
    held = [gate_ref.at[0], up_ref.at[0], gate_ref.at[1], up_ref.at[1]]
    held += [down_ref.at[0], down_ref.at[1]]
    copies = [
        pltpu.make_async_copy(hbm, ref, sems.at[i])
        for i, (hbm, ref) in enumerate(zip(weights, held, strict=True))
    ]
    for copy in copies:
        copy.start()
    rows, share = pieces[0].shape
    half = rows // 2
    width = gate_ref.shape[1]
    tile = 32

    for side in range(2):
        chosen = [(pieces[k], 0, k) for k in range(3)]
        chosen += [(pieces[3 + side], side * half, 3)]

        def norm(i, carry):
            at_row = pl.multiple_of(side * half + i * tile, tile)
            total = jnp.zeros((tile, share), F32)
            for ref, low, _ in chosen:
                v = ref[pl.ds(pl.multiple_of(at_row - low, tile), tile), :].astype(F32)
                total = total + v * v
            mean = jnp.sum(total, axis=1, keepdims=True) * (1.0 / width)
            scale = lax.rsqrt(mean + EPS)
            for ref, low, k in chosen:
                at = ids[k]
                v = ref[pl.ds(pl.multiple_of(at_row - low, tile), tile), :].astype(F32)
                v = v * scale * gain_ref[pl.ds(at, 1), :]
                column = pl.ds(pl.multiple_of(at * share, share), share)
                xs_ref[pl.ds(at_row, tile), column] = v.astype(BF16)
            return carry

        lax.fori_loop(0, half // tile, norm, 0)
    for k in range(2):
        copies[2 * k].wait()
        gate = jnp.dot(xs_ref[...], gate_ref[k], preferred_element_type=F32)
        copies[2 * k + 1].wait()
        up = jnp.dot(xs_ref[...], up_ref[k], preferred_element_type=F32)
        act_ref[k] = (gate / (1.0 + jnp.exp(-gate)) * up).astype(BF16)
    copies[4].wait()
    copies[5].wait()
    for k, ref in enumerate(outs):

        def body(i, carry):
            at_row = pl.ds(pl.multiple_of(i * half, half), half)
            column = pl.ds(pl.multiple_of(ids[4 + 2 * k + i] * share, share), share)
            total = jnp.dot(act_ref[0, at_row, :], down_ref[0, :, column], preferred_element_type=F32)
            total = total + jnp.dot(
                act_ref[1, at_row, :], down_ref[1, :, column], preferred_element_type=F32
            )
            ref[at_row, :] = total.astype(BF16)
            return carry

        lax.fori_loop(0, 2, body, 0)


def ffn(ids, gain, weights, pieces):
    rows, share = pieces[0].shape
    depth, width = weights[0].shape
    return pl.pallas_call(
        ffn_kernel,
        out_shape=(jax.ShapeDtypeStruct((rows, share), BF16),) * 4,
        in_specs=[SMEM_SPEC, VMEM_SPEC] + [HBM_SPEC] * 6 + [VMEM_SPEC] * len(pieces),
        out_specs=(VMEM_SPEC,) * 4,
        scratch_shapes=[
            pltpu.VMEM((rows, depth), BF16),
            pltpu.VMEM((2, rows, width), BF16),
            pltpu.VMEM((2, depth, width), BF16),
            pltpu.VMEM((2, depth, width), BF16),
            pltpu.VMEM((2, width, depth), BF16),
            pltpu.SemaphoreType.DMA((6,)),
        ],
        compiler_params=pltpu.CompilerParams(vmem_limit_bytes=40 * MIB),
    )(ids, gain, *weights, *pieces)


def gather_ring(own):
    half = own.shape[0] // 2
    below = send_z(own, 1)
    above = send_z(own, -1)
    far_a = send_z(below[:half], 1)
    far_b = send_z(above[half:], -1)
    return [own, below, above, far_a, far_b]


def relay_kernel(relay_ref, below_ref, above_ref, low_ref, high_ref):
    half = low_ref.shape[0]
    low = relay_ref[:half, :].astype(F32) + below_ref[:half, :].astype(F32)
    high = relay_ref[half:, :].astype(F32) + above_ref[half:, :].astype(F32)
    low_ref[...] = low.astype(BF16)
    high_ref[...] = high.astype(BF16)


def end_kernel(rest_ref, below_ref, above_ref, low_ref, high_ref, out_ref):
    half = low_ref.shape[0]
    total = rest_ref[...].astype(F32)
    first = total[:half] + above_ref[:half, :].astype(F32) + low_ref[...].astype(F32)
    second = total[half:] + below_ref[half:, :].astype(F32) + high_ref[...].astype(F32)
    out_ref[:half, :] = first.astype(BF16)
    out_ref[half:, :] = second.astype(BF16)


def local_call(kernel, args, heights):
    share = args[0].shape[1]
    return pl.pallas_call(
        kernel,
        out_shape=tuple(jax.ShapeDtypeStruct((height, share), BF16) for height in heights),
        in_specs=[VMEM_SPEC] * len(args),
        out_specs=(VMEM_SPEC,) * len(heights),
        compiler_params=pltpu.CompilerParams(vmem_limit_bytes=16 * MIB),
    )(*args)


def scatter_ring(up, down, relay, rest):
    rows = up.shape[0]
    half = rows // 2
    from_below = send_z(up, 1)
    from_above = send_z(down, -1)
    low, high = local_call(relay_kernel, (relay, from_below, from_above), (half, half))
    low = send_z(low, 1)
    high = send_z(high, -1)
    return local_call(end_kernel, (rest, from_below, from_above, low, high), (rows,))[0]


def local(
    tokens,
    segment_ids,
    routes,
    owners,
    gain_attn,
    w_query,
    w_kv,
    w_out,
    gain_moe,
    w_router,
    w_gate,
    w_up,
    w_down,
):
    seq_count = lax.axis_size("seq")
    ten_count = lax.axis_size("tensor")
    seq_rank = lax.axis_index("seq").astype(jnp.int32)
    ten_rank = lax.axis_index("tensor").astype(jnp.int32)
    rows, width = tokens.shape
    total = segment_ids.shape[0]
    w_out, w_gate, w_up, w_down = (
        pltpu.with_memory_space_constraint(w, pltpu.HBM) for w in (w_out, w_gate, w_up, w_down)
    )
    share = width // ten_count
    group = HEADS // KV_HEADS
    z = ten_rank // 2
    c = ten_rank - z * 2
    first = seq_rank * rows

    short_count = owners.shape[0] - 1
    labels = jnp.where(segment_ids < 0, short_count + 1, segment_ids)
    my_labels = lax.dynamic_slice_in_dim(labels, first, rows)
    seg_start = jnp.sum((labels[None, :] < my_labels[:, None]).astype(jnp.int32), axis=1)
    position = first + jnp.arange(rows, dtype=jnp.int32) - seg_start

    values = tokens.astype(F32)
    scale = lax.rsqrt(jnp.mean(values * values, axis=-1, keepdims=True) + EPS)
    normed = (values * scale * gain_attn).astype(BF16)
    half_dim = HEAD_DIM // 2
    freqs = THETA ** (-(jnp.arange(half_dim, dtype=F32) * 2.0) / HEAD_DIM)
    angles = position.astype(F32)[:, None] * freqs[None, :]
    cosine = jnp.cos(angles)
    sine = jnp.sin(angles)
    pairs = jnp.dot(normed, w_kv, preferred_element_type=F32)
    keys = rotate(pairs[:, :HEAD_DIM], cosine, sine).astype(BF16)
    kv_own = jnp.concatenate([keys, pairs[:, HEAD_DIM:].astype(BF16)], axis=1)
    queries = jnp.dot(normed, w_query, preferred_element_type=F32)
    q = jnp.concatenate(
        [
            rotate(queries[:, g * HEAD_DIM : (g + 1) * HEAD_DIM], cosine, sine).astype(BF16)
            for g in range(group)
        ],
        axis=0,
    )

    kv_all = lax.all_to_all(
        jnp.broadcast_to(kv_own[None], (seq_count,) + kv_own.shape), "seq", 0, 0, tiled=True
    ).reshape(total, kv_own.shape[1])

    g_sib, u_sib, d_sib = (send_core(w) for w in (w_gate, w_up, w_down))
    g_sib, u_sib, d_sib = (
        pltpu.with_memory_space_constraint(w, pltpu.HBM) for w in (g_sib, u_sib, d_sib)
    )
    weights = [w_gate, w_up, g_sib, u_sib, w_down, d_sib]

    ring = lax.rem(z + jnp.arange(NZ, dtype=jnp.int32), NZ) * 2
    other_c = 1 - c
    out_ids = jnp.concatenate([ring + c, ring + other_c])
    out_mine, out_sib = attend(
        out_ids, first.reshape(1), q, seg_start[:, None], kv_all, w_out, share
    )
    out_sib_r = send_core(out_sib)
    sums = [out_mine[d] + out_sib_r[d].astype(F32) for d in range(NZ)]
    attn_sum = sums[0]
    for d in (1, 3, 2):
        attn_sum = attn_sum + send_z(sums[d].astype(BF16), d).astype(F32)
    own_tokens = lax.dynamic_slice_in_dim(tokens, ten_rank * share, share, 1)
    residual = (own_tokens.astype(F32) + attn_sum).astype(BF16)

    sibling = send_core(residual)
    wide = jnp.where(
        c == 0,
        jnp.concatenate([residual, sibling], axis=1),
        jnp.concatenate([sibling, residual], axis=1),
    )

    slots = rows // 8
    holders = seq_count // EXPERTS
    expert_ids = jnp.arange(EXPERTS, dtype=jnp.int32)
    hit = (routes[:, 0:1] == expert_ids[None, :]) | (routes[:, 1:2] == expert_ids[None, :])
    index = jnp.arange(rows, dtype=jnp.int32)
    before = (index[:, None] > index[None, :]).astype(BF16)
    rank = jnp.dot(before, hit.astype(BF16), preferred_element_type=F32).astype(jnp.int32)
    slot_of = jnp.where(hit, rank, -1)
    slot_dup = jnp.repeat(slot_of.T, holders, axis=0)

    def pack(chunk):
        want = (2 * c + chunk) * slots + jnp.arange(slots, dtype=jnp.int32)
        return slot_dup[:, None, :] == want[None, :, None]

    picks = [pack(0), pack(1)]

    def exchange(flat):
        got = lax.all_to_all(
            flat.reshape(seq_count, slots, 2 * share), "seq", 0, 0, tiled=True
        )
        return got.reshape(seq_count * slots, 2 * share)

    def dispatch(pick):
        flat = pick.reshape(seq_count * slots, rows).astype(BF16)
        return exchange(jnp.dot(flat, wide, preferred_element_type=F32).astype(BF16))

    gain_wide = lax.dynamic_slice_in_dim(gain_moe, z * 2 * share, 2 * share)
    router = lax.dynamic_slice_in_dim(w_router, z * 2 * share, 2 * share)
    wide32 = wide.astype(F32)
    part = jnp.dot(
        wide32 * gain_wide, router, preferred_element_type=F32, precision=lax.Precision.HIGHEST
    )
    square = jnp.sum(wide32 * wide32, axis=1, keepdims=True)
    stats = jnp.concatenate([part, square, jnp.zeros((rows, 7), F32)], axis=1)
    stats = stats + lax.ppermute(stats, "tensor", [(t, t ^ 2) for t in range(ten_count)])
    stats = stats + lax.ppermute(stats, "tensor", [(t, t ^ 4) for t in range(ten_count)])
    logits = stats[:, :EXPERTS] * lax.rsqrt(stats[:, EXPERTS : EXPERTS + 1] / width + EPS)
    picked = routes[:, :, None] == expert_ids[None, None, :]
    chosen = jnp.sum(jnp.where(picked, logits[:, None, :], 0.0), axis=2)
    gates = jax.nn.softmax(chosen, axis=1)
    gate_of = jnp.sum(jnp.where(picked, gates[:, :, None], 0.0), axis=1)
    gate_dup = jnp.repeat(gate_of, holders, axis=1)

    gain_rows = gain_moe.reshape(NZ, 2 * share)
    hops = jnp.array([0, 3, 1, 2, 2, 1, 3, 2, 1, 3, 0, 0], jnp.int32)
    ids = lax.rem(z + hops, NZ)
    a_own = dispatch(picks[0])
    a_pieces = gather_ring(a_own)
    b_own = dispatch(picks[1])
    b_pieces = gather_ring(b_own)
    a_out = ffn(ids, gain_rows, weights, a_pieces)
    b_out = ffn(ids, gain_rows, weights, b_pieces)
    a_final = scatter_ring(*a_out)
    b_final = scatter_ring(*b_out)
    a_back = exchange(a_final)
    b_back = exchange(b_final)

    def combine(pick, back):
        weight = jnp.where(pick.transpose(2, 0, 1), gate_dup[:, :, None], 0.0)
        weight = weight.reshape(rows, seq_count * slots)
        high = weight.astype(BF16)
        low = (weight - high.astype(F32)).astype(BF16)
        return jnp.dot(high, back, preferred_element_type=F32) + jnp.dot(
            low, back, preferred_element_type=F32
        )

    mixture = combine(picks[0], a_back) + combine(picks[1], b_back)
    left, right = mixture[:, :share], mixture[:, share:]
    theirs = send_core(jnp.where(c == 0, right, left).astype(BF16))
    mine = jnp.where(c == 0, left, right)
    layer_out = (residual.astype(F32) + mine + theirs.astype(F32)).astype(BF16)

    owner_ext = jnp.concatenate([owners, jnp.full((1,), -1, jnp.int32)])
    label_ids = jnp.arange(short_count + 2, dtype=jnp.int32)
    owner_tok = jnp.sum(
        jnp.where(labels[:, None] == label_ids[None, :], owner_ext[None, :], 0), axis=1
    )
    held = (owner_tok == seq_rank).reshape(seq_count, rows)
    held_b = held.astype(BF16)
    inside = jnp.dot(held_b, before.T, preferred_element_type=F32)
    seq_index = jnp.arange(seq_count, dtype=jnp.int32)
    earlier = (seq_index[:, None] > seq_index[None, :]).astype(BF16)
    sizes = jnp.sum(held.astype(F32), axis=1).astype(BF16)
    ahead = jnp.dot(earlier, sizes[:, None], preferred_element_type=F32)
    slot = jnp.where(held, (inside + ahead).astype(jnp.int32), -1).reshape(1, total)
    places = jnp.arange(total, dtype=jnp.int32)
    take = (places[:, None] == slot).astype(BF16)
    cache = jnp.dot(take, kv_all, preferred_element_type=F32)
    return layer_out, cache.astype(BF16)


def solution(mesh):
    return jax.shard_map(
        local,
        mesh=mesh,
        in_specs=(
            P("seq", None),
            P(),
            P("seq", None),
            P(),
            P(),
            P(None, "tensor"),
            P(None, "tensor"),
            P("tensor", None),
            P(),
            P(),
            P(None, ("seq", "tensor")),
            P(None, ("seq", "tensor")),
            P(("seq", "tensor"), None),
        ),
        out_specs=(P("seq", "tensor"), P("seq", "tensor")),
        check_vma=False,
    )
```

```python
import jax
import jax.numpy as jnp
from jax import lax
from jax.experimental import pallas as pl
from jax.experimental.pallas import tpu as pltpu
from jax.sharding import PartitionSpec as P


HEADS = 32
KV_HEADS = 8
HEAD_DIM = 128
EXPERTS = 8
EPS = 1e-05
THETA = 1000000.0
FLOOR = -1e30
NZ = 4
MIB = 1024 * 1024
F32 = jnp.float32
BF16 = jnp.bfloat16


VMEM_SPEC = pl.BlockSpec(memory_space=pltpu.VMEM)
ANY_SPEC = pl.BlockSpec(memory_space=pl.ANY)
HBM_SPEC = pl.BlockSpec(memory_space=pltpu.HBM)
SMEM_SPEC = pl.BlockSpec(memory_space=pltpu.SMEM)


def z_perm(step):
    return [(2 * z + c, 2 * ((z + step) % NZ) + c) for z in range(NZ) for c in range(2)]


def core_perm():
    return [(t, t ^ 1) for t in range(2 * NZ)]


def send_z(value, step):
    return lax.ppermute(value, "tensor", z_perm(step))


def send_core(value):
    return lax.ppermute(value, "tensor", core_perm())


def rotate(values, cosine, sine):
    half = values.shape[-1] // 2
    first = values[..., :half]
    second = values[..., half:]
    return jnp.concatenate(
        [first * cosine - second * sine, second * cosine + first * sine], axis=-1
    )


def attention_kernel(ids, first_ref, q_ref, start_ref, kv_ref, w_hbm, mine_ref, sib_ref, w_ref, sem):
    copy = pltpu.make_async_copy(w_hbm, w_ref, sem)
    copy.start()
    rows, dim = start_ref.shape[0], HEAD_DIM
    group = q_ref.shape[0] // rows
    count = kv_ref.shape[0]
    query = first_ref[0] + lax.broadcasted_iota(jnp.int32, (rows, count), 0)
    key = lax.broadcasted_iota(jnp.int32, (rows, count), 1)
    mask = (key <= query) & (key >= start_ref[...])
    scale = HEAD_DIM ** (-0.5)
    heads = []
    for g in range(group):
        q = q_ref[g * rows : (g + 1) * rows, :]
        s = lax.dot_general(
            q, kv_ref[:, :dim], (((1,), (1,)), ((), ())), preferred_element_type=F32
        )
        s = jnp.where(mask, s * scale, FLOOR)
        w = jnp.exp(s - jnp.max(s, axis=1, keepdims=True))
        mass = jnp.sum(w, axis=1, keepdims=True)
        acc = jnp.dot(w.astype(BF16), kv_ref[:, dim:], preferred_element_type=F32)
        heads.append((acc / mass).astype(BF16))
    attended = jnp.concatenate(heads, axis=1)
    copy.wait()
    share = mine_ref.shape[2]

    def project(at):
        w = w_ref[:, pl.ds(pl.multiple_of(at * share, share), share)]
        return jnp.dot(attended, w, preferred_element_type=F32)

    def body(d, carry):
        sib_ref[d] = project(ids[4 + d]).astype(BF16)
        mine_ref[d] = project(ids[d])
        return carry

    lax.fori_loop(0, NZ, body, 0)


def attend(ids, first, q, start, kv, w_out, share):
    rows = start.shape[0]
    return pl.pallas_call(
        attention_kernel,
        out_shape=(
            jax.ShapeDtypeStruct((NZ, rows, share), F32),
            jax.ShapeDtypeStruct((NZ, rows, share), BF16),
        ),
        in_specs=[SMEM_SPEC, SMEM_SPEC, VMEM_SPEC, VMEM_SPEC, VMEM_SPEC, HBM_SPEC],
        out_specs=(VMEM_SPEC, VMEM_SPEC),
        scratch_shapes=[pltpu.VMEM(w_out.shape, BF16), pltpu.SemaphoreType.DMA],
        compiler_params=pltpu.CompilerParams(vmem_limit_bytes=24 * MIB),
    )(ids, first, q, start, kv, w_out)


def ffn_kernel(ids, gain_ref, *refs):
    weights = refs[:6]
    pieces = refs[6:-10]
    outs = refs[-10:-6]
    xs_ref, act_ref, gate_ref, up_ref, down_ref, sems = refs[-6:]
    held = [gate_ref.at[0], up_ref.at[0], gate_ref.at[1], up_ref.at[1]]
    held += [down_ref.at[0], down_ref.at[1]]
    copies = [
        pltpu.make_async_copy(hbm, ref, sems.at[i])
        for i, (hbm, ref) in enumerate(zip(weights, held, strict=True))
    ]
    for copy in copies:
        copy.start()
    rows, share = pieces[0].shape
    half = rows // 2
    width = gate_ref.shape[1]
    tile = 32

    for side in range(2):
        chosen = [(pieces[k], 0, k) for k in range(3)]
        chosen += [(pieces[3 + side], side * half, 3) if len(pieces) > 4 else (pieces[3], 0, 3)]

        def norm(i, carry):
            at_row = pl.multiple_of(side * half + i * tile, tile)
            total = jnp.zeros((tile, share), F32)
            for ref, low, _ in chosen:
                v = ref[pl.ds(pl.multiple_of(at_row - low, tile), tile), :].astype(F32)
                total = total + v * v
            mean = jnp.sum(total, axis=1, keepdims=True) * (1.0 / width)
            scale = lax.rsqrt(mean + EPS)
            for ref, low, k in chosen:
                at = ids[k]
                v = ref[pl.ds(pl.multiple_of(at_row - low, tile), tile), :].astype(F32)
                v = v * scale * gain_ref[pl.ds(at, 1), :]
                column = pl.ds(pl.multiple_of(at * share, share), share)
                xs_ref[pl.ds(at_row, tile), column] = v.astype(BF16)
            return carry

        lax.fori_loop(0, half // tile, norm, 0)
    for k in range(2):
        copies[2 * k].wait()
        gate = jnp.dot(xs_ref[...], gate_ref[k], preferred_element_type=F32)
        copies[2 * k + 1].wait()
        up = jnp.dot(xs_ref[...], up_ref[k], preferred_element_type=F32)
        act_ref[k] = (gate / (1.0 + jnp.exp(-gate)) * up).astype(BF16)
    copies[4].wait()
    copies[5].wait()
    for k, ref in enumerate(outs):

        def body(i, carry):
            at_row = pl.ds(pl.multiple_of(i * half, half), half)
            column = pl.ds(pl.multiple_of(ids[4 + 2 * k + i] * share, share), share)
            total = jnp.dot(act_ref[0, at_row, :], down_ref[0, :, column], preferred_element_type=F32)
            total = total + jnp.dot(
                act_ref[1, at_row, :], down_ref[1, :, column], preferred_element_type=F32
            )
            ref[at_row, :] = total.astype(BF16)
            return carry

        lax.fori_loop(0, 2, body, 0)


def ffn(ids, gain, weights, pieces):
    rows, share = pieces[0].shape
    depth, width = weights[0].shape
    return pl.pallas_call(
        ffn_kernel,
        out_shape=(jax.ShapeDtypeStruct((rows, share), BF16),) * 4,
        in_specs=[SMEM_SPEC, VMEM_SPEC] + [HBM_SPEC] * 6 + [VMEM_SPEC] * len(pieces),
        out_specs=(VMEM_SPEC,) * 4,
        scratch_shapes=[
            pltpu.VMEM((rows, depth), BF16),
            pltpu.VMEM((2, rows, width), BF16),
            pltpu.VMEM((2, depth, width), BF16),
            pltpu.VMEM((2, depth, width), BF16),
            pltpu.VMEM((2, width, depth), BF16),
            pltpu.SemaphoreType.DMA((6,)),
        ],
        compiler_params=pltpu.CompilerParams(vmem_limit_bytes=40 * MIB),
    )(ids, gain, *weights, *pieces)


def in_vmem(value):
    return pltpu.with_memory_space_constraint(value, pltpu.VMEM)


def in_hbm(value):
    return pltpu.with_memory_space_constraint(value, pltpu.HBM)


def gather_direct(own):
    below = in_vmem(send_z(own, 1))
    above = in_vmem(send_z(own, -1))
    far = in_vmem(send_z(own, 2))
    return [own, below, above, far]


def split_kernel(below_ref, above_ref, low_ref, high_ref):
    half = low_ref.shape[0]
    low_ref[...] = below_ref[:half, :]
    high_ref[...] = above_ref[half:, :]


def gather_ring(own):
    half = own.shape[0] // 2
    below = in_vmem(send_z(own, 1))
    above = in_vmem(send_z(own, -1))
    low, high = local_call(split_kernel, (below, above), (half, half))
    far_a = in_vmem(send_z(low, 1))
    far_b = in_vmem(send_z(high, -1))
    return [own, below, above, far_a, far_b]


def relay_kernel(relay_ref, below_ref, above_ref, low_ref, high_ref):
    half = low_ref.shape[0]
    low = relay_ref[:half, :].astype(F32) + below_ref[:half, :].astype(F32)
    high = relay_ref[half:, :].astype(F32) + above_ref[half:, :].astype(F32)
    low_ref[...] = low.astype(BF16)
    high_ref[...] = high.astype(BF16)


def end_kernel(rest_ref, below_ref, above_ref, low_ref, high_ref, out_ref):
    half = low_ref.shape[0]
    total = rest_ref[...].astype(F32)
    first = total[:half] + above_ref[:half, :].astype(F32) + low_ref[...].astype(F32)
    second = total[half:] + below_ref[half:, :].astype(F32) + high_ref[...].astype(F32)
    out_ref[:half, :] = first.astype(BF16)
    out_ref[half:, :] = second.astype(BF16)


def local_call(kernel, args, heights):
    share = args[0].shape[1]
    return pl.pallas_call(
        kernel,
        out_shape=tuple(jax.ShapeDtypeStruct((height, share), BF16) for height in heights),
        in_specs=[VMEM_SPEC] * len(args),
        out_specs=(VMEM_SPEC,) * len(heights),
        compiler_params=pltpu.CompilerParams(vmem_limit_bytes=16 * MIB),
    )(*args)


def sum_kernel(*refs):
    total = refs[0][...].astype(F32)
    for ref in refs[1:-1]:
        total = total + ref[...].astype(F32)
    refs[-1][...] = total.astype(BF16)


def scatter_direct(near, above, far, rest):
    moved = [in_vmem(send_z(v, d)) for v, d in ((near, 1), (above, -1), (far, 2))]
    return local_call(sum_kernel, (in_hbm(rest), *moved), (rest.shape[0],))[0]


def scatter_ring(up, down, relay, rest):
    rows = up.shape[0]
    half = rows // 2
    from_below = in_vmem(send_z(up, 1))
    from_above = in_vmem(send_z(down, -1))
    low, high = local_call(
        relay_kernel, (in_hbm(relay), from_below, from_above), (half, half)
    )
    low = in_hbm(send_z(in_hbm(low), 1))
    high = in_hbm(send_z(in_hbm(high), -1))
    moved = (from_below, from_above, low, high)
    return local_call(end_kernel, (in_hbm(rest), *moved), (rows,))[0]


def cache_kernel(slot_ref, kv_ref, out_ref):
    rows, total = out_ref.shape[0], kv_ref.shape[0]
    place = pl.program_id(0) * rows + lax.broadcasted_iota(jnp.int32, (rows, total), 0)
    take = jnp.where(place == slot_ref[...], 1.0, 0.0).astype(BF16)
    out_ref[...] = jnp.dot(take, kv_ref[...], preferred_element_type=F32).astype(BF16)


def fill_cache(slot, kv):
    total, width = kv.shape
    rows = 256
    return pl.pallas_call(
        cache_kernel,
        grid=(total // rows,),
        out_shape=jax.ShapeDtypeStruct((total, width), BF16),
        in_specs=[
            pl.BlockSpec((1, total), lambda i: (0, 0)),
            pl.BlockSpec((total, width), lambda i: (0, 0)),
        ],
        out_specs=pl.BlockSpec((rows, width), lambda i: (i, 0)),
        compiler_params=pltpu.CompilerParams(vmem_limit_bytes=12 * MIB),
    )(slot, kv)


def local(
    tokens,
    segment_ids,
    routes,
    owners,
    gain_attn,
    w_query,
    w_kv,
    w_out,
    gain_moe,
    w_router,
    w_gate,
    w_up,
    w_down,
):
    seq_count = lax.axis_size("seq")
    ten_count = lax.axis_size("tensor")
    seq_rank = lax.axis_index("seq").astype(jnp.int32)
    ten_rank = lax.axis_index("tensor").astype(jnp.int32)
    rows, width = tokens.shape
    total = segment_ids.shape[0]
    w_out, w_gate, w_up, w_down = (
        pltpu.with_memory_space_constraint(w, pltpu.HBM) for w in (w_out, w_gate, w_up, w_down)
    )
    share = width // ten_count
    group = HEADS // KV_HEADS
    z = ten_rank // 2
    c = ten_rank - z * 2
    first = seq_rank * rows

    short_count = owners.shape[0] - 1
    labels = jnp.where(segment_ids < 0, short_count + 1, segment_ids)
    my_labels = lax.dynamic_slice_in_dim(labels, first, rows)
    seg_start = jnp.sum((labels[None, :] < my_labels[:, None]).astype(jnp.int32), axis=1)
    position = first + jnp.arange(rows, dtype=jnp.int32) - seg_start

    values = tokens.astype(F32)
    scale = lax.rsqrt(jnp.mean(values * values, axis=-1, keepdims=True) + EPS)
    normed = (values * scale * gain_attn).astype(BF16)
    half_dim = HEAD_DIM // 2
    freqs = THETA ** (-(jnp.arange(half_dim, dtype=F32) * 2.0) / HEAD_DIM)
    angles = position.astype(F32)[:, None] * freqs[None, :]
    cosine = jnp.cos(angles)
    sine = jnp.sin(angles)
    pairs = jnp.dot(normed, w_kv, preferred_element_type=F32)
    keys = rotate(pairs[:, :HEAD_DIM], cosine, sine).astype(BF16)
    kv_own = jnp.concatenate([keys, pairs[:, HEAD_DIM:].astype(BF16)], axis=1)
    queries = jnp.dot(normed, w_query, preferred_element_type=F32)
    q = jnp.concatenate(
        [
            rotate(queries[:, g * HEAD_DIM : (g + 1) * HEAD_DIM], cosine, sine).astype(BF16)
            for g in range(group)
        ],
        axis=0,
    )

    kv_all = lax.all_to_all(
        jnp.broadcast_to(kv_own[None], (seq_count,) + kv_own.shape), "seq", 0, 0, tiled=True
    ).reshape(total, kv_own.shape[1])

    g_sib, u_sib, d_sib = (send_core(w) for w in (w_gate, w_up, w_down))
    g_sib, u_sib, d_sib = (
        pltpu.with_memory_space_constraint(w, pltpu.HBM) for w in (g_sib, u_sib, d_sib)
    )
    weights = [w_gate, w_up, g_sib, u_sib, w_down, d_sib]

    ring = lax.rem(z + jnp.arange(NZ, dtype=jnp.int32), NZ) * 2
    other_c = 1 - c
    out_ids = jnp.concatenate([ring + c, ring + other_c])
    out_mine, out_sib = attend(
        out_ids, first.reshape(1), q, seg_start[:, None], kv_all, w_out, share
    )
    out_sib_r = send_core(out_sib)
    sums = [out_mine[d] + out_sib_r[d].astype(F32) for d in range(NZ)]
    attn_sum = sums[0]
    for d in (1, 3, 2):
        attn_sum = attn_sum + send_z(sums[d].astype(BF16), d).astype(F32)
    own_tokens = lax.dynamic_slice_in_dim(tokens, ten_rank * share, share, 1)
    residual = (own_tokens.astype(F32) + attn_sum).astype(BF16)

    sibling = send_core(residual)
    wide = jnp.where(
        c == 0,
        jnp.concatenate([residual, sibling], axis=1),
        jnp.concatenate([sibling, residual], axis=1),
    )

    slots = rows // 8
    holders = seq_count // EXPERTS
    expert_ids = jnp.arange(EXPERTS, dtype=jnp.int32)
    hit = (routes[:, 0:1] == expert_ids[None, :]) | (routes[:, 1:2] == expert_ids[None, :])
    index = jnp.arange(rows, dtype=jnp.int32)
    before = (index[:, None] > index[None, :]).astype(BF16)
    rank = jnp.dot(before, hit.astype(BF16), preferred_element_type=F32).astype(jnp.int32)
    slot_of = jnp.where(hit, rank, -1)
    slot_dup = jnp.repeat(slot_of.T, holders, axis=0)

    def pack(chunk):
        want = (2 * c + chunk) * slots + jnp.arange(slots, dtype=jnp.int32)
        return slot_dup[:, None, :] == want[None, :, None]

    picks = [pack(0), pack(1)]

    def exchange(flat):
        got = lax.all_to_all(
            flat.reshape(seq_count, slots, 2 * share), "seq", 0, 0, tiled=True
        )
        return got.reshape(seq_count * slots, 2 * share)

    def dispatch(pick):
        flat = pick.reshape(seq_count * slots, rows).astype(BF16)
        return exchange(jnp.dot(flat, wide, preferred_element_type=F32).astype(BF16))

    gain_wide = lax.dynamic_slice_in_dim(gain_moe, z * 2 * share, 2 * share)
    router = lax.dynamic_slice_in_dim(w_router, z * 2 * share, 2 * share)
    wide32 = wide.astype(F32)
    part = jnp.dot(
        wide32 * gain_wide, router, preferred_element_type=F32, precision=lax.Precision.HIGHEST
    )
    square = jnp.sum(wide32 * wide32, axis=1, keepdims=True)
    stats = jnp.concatenate([part, square, jnp.zeros((rows, 7), F32)], axis=1)
    stats = stats + lax.ppermute(stats, "tensor", [(t, t ^ 2) for t in range(ten_count)])
    stats = stats + lax.ppermute(stats, "tensor", [(t, t ^ 4) for t in range(ten_count)])
    logits = stats[:, :EXPERTS] * lax.rsqrt(stats[:, EXPERTS : EXPERTS + 1] / width + EPS)
    picked = routes[:, :, None] == expert_ids[None, None, :]
    chosen = jnp.sum(jnp.where(picked, logits[:, None, :], 0.0), axis=2)
    gates = jax.nn.softmax(chosen, axis=1)
    gate_of = jnp.sum(jnp.where(picked, gates[:, :, None], 0.0), axis=1)
    gate_dup = jnp.repeat(gate_of, holders, axis=1)

    gain_rows = gain_moe.reshape(NZ, 2 * share)
    from_z = [0, 3, 1, 2]
    direct_ids = lax.rem(z + jnp.array(from_z + [1, 1, 3, 3, 2, 2, 0, 0], jnp.int32), NZ)
    ring_ids = lax.rem(z + jnp.array(from_z + [2, 1, 3, 2, 1, 3, 0, 0], jnp.int32), NZ)
    a_own = dispatch(picks[0])
    a_pieces = gather_ring(a_own)
    b_own = dispatch(picks[1])
    b_pieces = gather_direct(b_own)
    a_out = ffn(direct_ids, gain_rows, weights, a_pieces)
    b_out = ffn(ring_ids, gain_rows, weights, b_pieces)
    a_final = scatter_direct(*a_out)
    b_final = scatter_ring(*b_out)
    a_back = exchange(a_final)
    b_back = exchange(b_final)

    def combine(pick, back):
        weight = jnp.where(pick.transpose(2, 0, 1), gate_dup[:, :, None], 0.0)
        weight = weight.reshape(rows, seq_count * slots)
        high = weight.astype(BF16)
        low = (weight - high.astype(F32)).astype(BF16)
        return jnp.dot(high, back, preferred_element_type=F32) + jnp.dot(
            low, back, preferred_element_type=F32
        )

    mixture = combine(picks[0], a_back) + combine(picks[1], b_back)
    left, right = mixture[:, :share], mixture[:, share:]
    theirs = send_core(jnp.where(c == 0, right, left).astype(BF16))
    mine = jnp.where(c == 0, left, right)
    layer_out = (residual.astype(F32) + mine + theirs.astype(F32)).astype(BF16)

    owner_ext = jnp.concatenate([owners, jnp.full((1,), -1, jnp.int32)])
    label_ids = jnp.arange(short_count + 2, dtype=jnp.int32)
    owner_tok = jnp.sum(
        jnp.where(labels[:, None] == label_ids[None, :], owner_ext[None, :], 0), axis=1
    )
    held = (owner_tok == seq_rank).reshape(seq_count, rows)
    held_b = held.astype(BF16)
    inside = jnp.dot(held_b, before.T, preferred_element_type=F32)
    seq_index = jnp.arange(seq_count, dtype=jnp.int32)
    earlier = (seq_index[:, None] > seq_index[None, :]).astype(BF16)
    sizes = jnp.sum(held.astype(F32), axis=1).astype(BF16)
    ahead = jnp.dot(earlier, sizes[:, None], preferred_element_type=F32)
    slot = jnp.where(held, (inside + ahead).astype(jnp.int32), -1).reshape(1, total)
    cache = fill_cache(slot, kv_all)
    return layer_out, cache


def solution(mesh):
    return jax.shard_map(
        local,
        mesh=mesh,
        in_specs=(
            P("seq", None),
            P(),
            P("seq", None),
            P(),
            P(),
            P(None, "tensor"),
            P(None, "tensor"),
            P("tensor", None),
            P(),
            P(),
            P(None, ("seq", "tensor")),
            P(None, ("seq", "tensor")),
            P(("seq", "tensor"), None),
        ),
        out_specs=(P("seq", "tensor"), P("seq", "tensor")),
        check_vma=False,
    )
```

```python
import functools

import jax
import jax.numpy as jnp
from jax import lax
from jax.experimental import pallas as pl
from jax.experimental.pallas import tpu as pltpu
from jax.sharding import PartitionSpec as P


HEADS = 32
KV_HEADS = 8
HEAD_DIM = 128
EXPERTS = 8
EPS = 1e-05
THETA = 1000000.0
FLOOR = -1e30
NZ = 4
MIB = 1024 * 1024
F32 = jnp.float32
BF16 = jnp.bfloat16


VMEM_SPEC = pl.BlockSpec(memory_space=pltpu.VMEM)
ANY_SPEC = pl.BlockSpec(memory_space=pl.ANY)
HBM_SPEC = pl.BlockSpec(memory_space=pltpu.HBM)
SMEM_SPEC = pl.BlockSpec(memory_space=pltpu.SMEM)


def z_perm(step):
    return [(2 * z + c, 2 * ((z + step) % NZ) + c) for z in range(NZ) for c in range(2)]


def core_perm():
    return [(t, t ^ 1) for t in range(2 * NZ)]


def send_z(value, step):
    return lax.ppermute(value, "tensor", z_perm(step))


def send_core(value):
    return lax.ppermute(value, "tensor", core_perm())


def rotate(values, cosine, sine):
    half = values.shape[-1] // 2
    first = values[..., :half]
    second = values[..., half:]
    return jnp.concatenate(
        [first * cosine - second * sine, second * cosine + first * sine], axis=-1
    )


def attention_kernel(ids, first_ref, q_ref, start_ref, kv_ref, w_hbm, mine_ref, sib_ref, w_ref, sem):
    copy = pltpu.make_async_copy(w_hbm, w_ref, sem)
    copy.start()
    rows, dim = start_ref.shape[0], HEAD_DIM
    group = q_ref.shape[0] // rows
    count = kv_ref.shape[0]
    both = 2 * rows
    inner = lax.broadcasted_iota(jnp.int32, (both, count), 0)
    query = first_ref[0] + jnp.where(inner >= rows, inner - rows, inner)
    key = lax.broadcasted_iota(jnp.int32, (both, count), 1)
    start = jnp.concatenate([start_ref[...], start_ref[...]], axis=0)
    mask = (key <= query) & (key >= start)
    scale = HEAD_DIM ** (-0.5)
    heads = []
    for g in range(0, group, 2):
        q = q_ref[g * rows : (g + 2) * rows, :]
        s = lax.dot_general(
            q, kv_ref[:, :dim], (((1,), (1,)), ((), ())), preferred_element_type=F32
        )
        s = jnp.where(mask, s * scale, FLOOR)
        w = jnp.exp(s - jnp.max(s, axis=1, keepdims=True))
        mass = jnp.sum(w, axis=1, keepdims=True)
        acc = jnp.dot(w.astype(BF16), kv_ref[:, dim:], preferred_element_type=F32)
        acc = (acc / mass).astype(BF16)
        heads += [acc[:rows], acc[rows:]]
    attended = jnp.concatenate(heads, axis=1)
    copy.wait()
    share = mine_ref.shape[2]

    def project(at):
        w = w_ref[:, pl.ds(pl.multiple_of(at * share, share), share)]
        return jnp.dot(attended, w, preferred_element_type=F32)

    def body(d, carry):
        sib_ref[d] = project(ids[4 + d]).astype(BF16)
        mine_ref[d] = project(ids[d])
        return carry

    lax.fori_loop(0, NZ, body, 0)


def attend(ids, first, q, start, kv, w_out, share):
    rows = start.shape[0]
    return pl.pallas_call(
        attention_kernel,
        out_shape=(
            jax.ShapeDtypeStruct((NZ, rows, share), F32),
            jax.ShapeDtypeStruct((NZ, rows, share), BF16),
        ),
        in_specs=[SMEM_SPEC, SMEM_SPEC, VMEM_SPEC, VMEM_SPEC, VMEM_SPEC, HBM_SPEC],
        out_specs=(VMEM_SPEC, VMEM_SPEC),
        scratch_shapes=[pltpu.VMEM(w_out.shape, BF16), pltpu.SemaphoreType.DMA],
        compiler_params=pltpu.CompilerParams(vmem_limit_bytes=24 * MIB),
    )(ids, first, q, start, kv, w_out)


def ffn_kernel(count, pieces_to_outs, ids, gain_ref, *refs):
    pieces, refs = refs[:count], refs[count:]
    copies = []
    if len(refs) > 9:
        sources, outs, held, (xs_ref, act_ref, sems) = refs[:6], refs[6:10], refs[10:13], refs[13:]
        gate_ref, up_ref, down_ref = held
        places = [gate_ref.at[0], up_ref.at[0], gate_ref.at[1], up_ref.at[1]]
        places += [down_ref.at[0], down_ref.at[1]]
        copies = [
            pltpu.make_async_copy(source, ref, sems.at[i])
            for i, (source, ref) in enumerate(zip(sources, places, strict=True))
        ]
    else:
        gate_ref, up_ref, down_ref = refs[:3]
        outs, (xs_ref, act_ref) = refs[3:7], refs[7:]
    for copy in copies[:3]:
        copy.start()

    def arrived(i):
        if copies:
            copies[i].wait()
            if i + 3 < len(copies):
                copies[i + 3].start()

    rows, share = pieces[0].shape
    half = rows // 2
    width = gate_ref.shape[1]
    tile = 32

    for side in range(2):
        chosen = [(pieces[k], 0, k) for k in range(3)]
        chosen += [(pieces[3 + side], side * half, 3) if len(pieces) > 4 else (pieces[3], 0, 3)]

        def norm(i, carry):
            at_row = pl.multiple_of(side * half + i * tile, tile)
            total = jnp.zeros((tile, share), F32)
            for ref, low, _ in chosen:
                v = ref[pl.ds(pl.multiple_of(at_row - low, tile), tile), :].astype(F32)
                total = total + v * v
            mean = jnp.sum(total, axis=1, keepdims=True) * (1.0 / width)
            scale = lax.rsqrt(mean + EPS)
            for ref, low, k in chosen:
                at = ids[k]
                v = ref[pl.ds(pl.multiple_of(at_row - low, tile), tile), :].astype(F32)
                v = v * scale * gain_ref[pl.ds(at, 1), :]
                column = pl.ds(pl.multiple_of(at * share, share), share)
                xs_ref[pl.ds(at_row, tile), column] = v.astype(BF16)
            return carry

        lax.fori_loop(0, half // tile, norm, 0)

    for k in range(2):
        arrived(2 * k)
        gate = jnp.dot(xs_ref[...], gate_ref[k], preferred_element_type=F32)
        arrived(2 * k + 1)
        up = jnp.dot(xs_ref[...], up_ref[k], preferred_element_type=F32)
        act_ref[k] = (gate / (1.0 + jnp.exp(-gate)) * up).astype(BF16)
    arrived(4)
    arrived(5)
    for d in (2, 1, 3, 0):
        column = pl.ds(pl.multiple_of(ids[4 + d] * share, share), share)
        total = jnp.dot(act_ref[0], down_ref[0, :, column], preferred_element_type=F32)
        total = total + jnp.dot(act_ref[1], down_ref[1, :, column], preferred_element_type=F32)
        total = total.astype(BF16)
        for part in range(2):
            at_row = slice(part * half, (part + 1) * half)
            outs[pieces_to_outs[d][part]][at_row, :] = total[at_row, :]


def ffn(ids, gain, weights, pieces, targets):
    rows, share = pieces[0].shape
    depth, width = weights[0].shape[-2:]
    outs = (jax.ShapeDtypeStruct((rows, share), BF16),) * 4
    scratch = [pltpu.VMEM((rows, depth), BF16), pltpu.VMEM((2, rows, width), BF16)]
    spec = VMEM_SPEC
    if len(weights) == 6:
        shapes = (weights[0].shape, weights[1].shape, weights[4].shape)
        outs += tuple(jax.ShapeDtypeStruct((2,) + shape, BF16) for shape in shapes)
        scratch.append(pltpu.SemaphoreType.DMA((6,)))
        spec = HBM_SPEC
    return pl.pallas_call(
        functools.partial(ffn_kernel, len(pieces), targets),
        out_shape=outs,
        in_specs=[SMEM_SPEC] + [VMEM_SPEC] * (1 + len(pieces)) + [spec] * len(weights),
        out_specs=(VMEM_SPEC,) * len(outs),
        scratch_shapes=scratch,
        compiler_params=pltpu.CompilerParams(vmem_limit_bytes=16 * MIB),
    )(ids, gain, *pieces, *weights)


def in_vmem(value):
    return pltpu.with_memory_space_constraint(value, pltpu.VMEM)


def in_hbm(value):
    return pltpu.with_memory_space_constraint(value, pltpu.HBM)


def gather_direct(own):
    below = in_vmem(send_z(own, 1))
    above = in_vmem(send_z(own, -1))
    far = in_vmem(send_z(own, 2))
    return [own, below, above, far]


def split_kernel(below_ref, above_ref, low_ref, high_ref):
    half = low_ref.shape[0]
    low_ref[...] = below_ref[:half, :]
    high_ref[...] = above_ref[half:, :]


def gather_ring(own):
    half = own.shape[0] // 2
    below = in_vmem(send_z(own, 1))
    above = in_vmem(send_z(own, -1))
    low, high = local_call(split_kernel, (below, above), (half, half))
    far_a = in_vmem(send_z(low, 1))
    far_b = in_vmem(send_z(high, -1))
    return [own, below, above, far_a, far_b]


def relay_kernel(relay_ref, below_ref, above_ref, low_ref, high_ref):
    half = low_ref.shape[0]
    low = relay_ref[:half, :].astype(F32) + below_ref[:half, :].astype(F32)
    high = relay_ref[half:, :].astype(F32) + above_ref[half:, :].astype(F32)
    low_ref[...] = low.astype(BF16)
    high_ref[...] = high.astype(BF16)


def end_kernel(rest_ref, below_ref, above_ref, low_ref, high_ref, out_ref):
    half = low_ref.shape[0]
    total = rest_ref[...].astype(F32)
    first = total[:half] + above_ref[:half, :].astype(F32) + low_ref[...].astype(F32)
    second = total[half:] + below_ref[half:, :].astype(F32) + high_ref[...].astype(F32)
    out_ref[:half, :] = first.astype(BF16)
    out_ref[half:, :] = second.astype(BF16)


def local_call(kernel, args, heights):
    share = args[0].shape[1]
    return pl.pallas_call(
        kernel,
        out_shape=tuple(jax.ShapeDtypeStruct((height, share), BF16) for height in heights),
        in_specs=[VMEM_SPEC] * len(args),
        out_specs=(VMEM_SPEC,) * len(heights),
        compiler_params=pltpu.CompilerParams(vmem_limit_bytes=16 * MIB),
    )(*args)


def sum_kernel(*refs):
    total = refs[0][...].astype(F32)
    for ref in refs[1:-1]:
        total = total + ref[...].astype(F32)
    refs[-1][...] = total.astype(BF16)


def scatter_direct(near, above, far, rest):
    moved = [in_vmem(send_z(v, d)) for v, d in ((near, 1), (above, -1), (far, 2))]
    return local_call(sum_kernel, (in_hbm(rest), *moved), (rest.shape[0],))[0]


def scatter_ring(up, down, relay, rest):
    rows = up.shape[0]
    half = rows // 2
    from_below = in_vmem(send_z(up, 1))
    from_above = in_vmem(send_z(down, -1))
    low, high = local_call(
        relay_kernel, (in_hbm(relay), from_below, from_above), (half, half)
    )
    low = in_hbm(send_z(in_hbm(low), 1))
    high = in_hbm(send_z(in_hbm(high), -1))
    moved = (from_below, from_above, low, high)
    return local_call(end_kernel, (in_hbm(rest), *moved), (rows,))[0]


def cache_kernel(slot_ref, kv_ref, out_ref):
    rows, total = out_ref.shape[0], kv_ref.shape[0]
    place = pl.program_id(0) * rows + lax.broadcasted_iota(jnp.int32, (rows, total), 0)
    take = jnp.where(place == slot_ref[...], 1.0, 0.0).astype(BF16)
    out_ref[...] = jnp.dot(take, kv_ref[...], preferred_element_type=F32).astype(BF16)


def fill_cache(slot, kv):
    total, width = kv.shape
    rows = 256
    return pl.pallas_call(
        cache_kernel,
        grid=(total // rows,),
        out_shape=jax.ShapeDtypeStruct((total, width), BF16),
        in_specs=[
            pl.BlockSpec((1, total), lambda i: (0, 0)),
            pl.BlockSpec((total, width), lambda i: (0, 0)),
        ],
        out_specs=pl.BlockSpec((rows, width), lambda i: (i, 0)),
        compiler_params=pltpu.CompilerParams(vmem_limit_bytes=12 * MIB),
    )(slot, kv)


def local(
    tokens,
    segment_ids,
    routes,
    owners,
    gain_attn,
    w_query,
    w_kv,
    w_out,
    gain_moe,
    w_router,
    w_gate,
    w_up,
    w_down,
):
    seq_count = lax.axis_size("seq")
    ten_count = lax.axis_size("tensor")
    seq_rank = lax.axis_index("seq").astype(jnp.int32)
    ten_rank = lax.axis_index("tensor").astype(jnp.int32)
    rows, width = tokens.shape
    total = segment_ids.shape[0]
    w_out, w_gate, w_up, w_down = (
        pltpu.with_memory_space_constraint(w, pltpu.HBM) for w in (w_out, w_gate, w_up, w_down)
    )
    share = width // ten_count
    group = HEADS // KV_HEADS
    z = ten_rank // 2
    c = ten_rank - z * 2
    first = seq_rank * rows

    short_count = owners.shape[0] - 1
    labels = jnp.where(segment_ids < 0, short_count + 1, segment_ids)
    my_labels = lax.dynamic_slice_in_dim(labels, first, rows)
    seg_start = jnp.sum((labels[None, :] < my_labels[:, None]).astype(jnp.int32), axis=1)
    position = first + jnp.arange(rows, dtype=jnp.int32) - seg_start

    values = tokens.astype(F32)
    scale = lax.rsqrt(jnp.mean(values * values, axis=-1, keepdims=True) + EPS)
    normed = (values * scale * gain_attn).astype(BF16)
    half_dim = HEAD_DIM // 2
    freqs = THETA ** (-(jnp.arange(half_dim, dtype=F32) * 2.0) / HEAD_DIM)
    angles = position.astype(F32)[:, None] * freqs[None, :]
    cosine = jnp.cos(angles)
    sine = jnp.sin(angles)
    pairs = jnp.dot(normed, w_kv, preferred_element_type=F32)
    keys = rotate(pairs[:, :HEAD_DIM], cosine, sine).astype(BF16)
    kv_own = jnp.concatenate([keys, pairs[:, HEAD_DIM:].astype(BF16)], axis=1)
    queries = jnp.dot(normed, w_query, preferred_element_type=F32)
    q = jnp.concatenate(
        [
            rotate(queries[:, g * HEAD_DIM : (g + 1) * HEAD_DIM], cosine, sine).astype(BF16)
            for g in range(group)
        ],
        axis=0,
    )

    kv_all = lax.all_to_all(
        jnp.broadcast_to(kv_own[None], (seq_count,) + kv_own.shape), "seq", 0, 0, tiled=True
    ).reshape(total, kv_own.shape[1])

    g_sib, u_sib, d_sib = (send_core(w) for w in (w_gate, w_up, w_down))
    g_sib, u_sib, d_sib = (
        pltpu.with_memory_space_constraint(w, pltpu.HBM) for w in (g_sib, u_sib, d_sib)
    )
    weights = [w_gate, w_up, g_sib, u_sib, w_down, d_sib]

    ring = lax.rem(z + jnp.arange(NZ, dtype=jnp.int32), NZ) * 2
    other_c = 1 - c
    out_ids = jnp.concatenate([ring + c, ring + other_c])
    out_mine, out_sib = attend(
        out_ids, first.reshape(1), q, seg_start[:, None], kv_all, w_out, share
    )
    out_sib_r = send_core(out_sib)
    sums = [out_mine[d] + out_sib_r[d].astype(F32) for d in range(NZ)]
    attn_sum = sums[0]
    for d in (1, 3, 2):
        attn_sum = attn_sum + send_z(sums[d].astype(BF16), d).astype(F32)
    own_tokens = lax.dynamic_slice_in_dim(tokens, ten_rank * share, share, 1)
    residual = (own_tokens.astype(F32) + attn_sum).astype(BF16)

    sibling = send_core(residual)
    wide = jnp.where(
        c == 0,
        jnp.concatenate([residual, sibling], axis=1),
        jnp.concatenate([sibling, residual], axis=1),
    )

    slots = rows // 8
    holders = seq_count // EXPERTS
    expert_ids = jnp.arange(EXPERTS, dtype=jnp.int32)
    hit = (routes[:, 0:1] == expert_ids[None, :]) | (routes[:, 1:2] == expert_ids[None, :])
    index = jnp.arange(rows, dtype=jnp.int32)
    before = (index[:, None] > index[None, :]).astype(BF16)
    rank = jnp.dot(before, hit.astype(BF16), preferred_element_type=F32).astype(jnp.int32)
    slot_of = jnp.where(hit, rank, -1)
    slot_dup = jnp.repeat(slot_of.T, holders, axis=0)

    def pack(chunk):
        want = (2 * c + chunk) * slots + jnp.arange(slots, dtype=jnp.int32)
        return slot_dup[:, None, :] == want[None, :, None]

    picks = [pack(0), pack(1)]

    def exchange(flat):
        got = lax.all_to_all(
            flat.reshape(seq_count, slots, 2 * share), "seq", 0, 0, tiled=True
        )
        return got.reshape(seq_count * slots, 2 * share)

    def dispatch(pick):
        flat = pick.reshape(seq_count * slots, rows).astype(BF16)
        return exchange(jnp.dot(flat, wide, preferred_element_type=F32).astype(BF16))

    gain_wide = lax.dynamic_slice_in_dim(gain_moe, z * 2 * share, 2 * share)
    router = lax.dynamic_slice_in_dim(w_router, z * 2 * share, 2 * share)
    wide32 = wide.astype(F32)
    part = jnp.dot(
        wide32 * gain_wide, router, preferred_element_type=F32, precision=lax.Precision.HIGHEST
    )
    square = jnp.sum(wide32 * wide32, axis=1, keepdims=True)
    stats = jnp.concatenate([part, square, jnp.zeros((rows, 7), F32)], axis=1)
    stats = stats + lax.ppermute(stats, "tensor", [(t, t ^ 2) for t in range(ten_count)])
    stats = stats + lax.ppermute(stats, "tensor", [(t, t ^ 4) for t in range(ten_count)])
    logits = stats[:, :EXPERTS] * lax.rsqrt(stats[:, EXPERTS : EXPERTS + 1] / width + EPS)
    picked = routes[:, :, None] == expert_ids[None, None, :]
    chosen = jnp.sum(jnp.where(picked, logits[:, None, :], 0.0), axis=2)
    gates = jax.nn.softmax(chosen, axis=1)
    gate_of = jnp.sum(jnp.where(picked, gates[:, :, None], 0.0), axis=1)
    gate_dup = jnp.repeat(gate_of, holders, axis=1)

    gain_rows = gain_moe.reshape(NZ, 2 * share)
    ids = lax.rem(z + jnp.array([0, 3, 1, 2, 0, 1, 2, 3], jnp.int32), NZ)
    direct_outs = ((3, 3), (0, 0), (2, 2), (1, 1))
    ring_outs = ((3, 3), (2, 0), (0, 1), (1, 2))
    a_own = dispatch(picks[0])
    a_pieces = gather_ring(a_own)
    b_own = dispatch(picks[1])
    b_pieces = gather_direct(b_own)
    *a_out, g_held, u_held, d_held = ffn(ids, gain_rows, weights, a_pieces, direct_outs)
    held = [in_vmem(w) for w in (g_held, u_held, d_held)]
    b_out = ffn(ids, gain_rows, held, b_pieces, ring_outs)
    a_final = scatter_direct(*a_out)
    b_final = scatter_ring(*b_out)
    a_back = exchange(a_final)
    b_back = exchange(b_final)

    def combine(pick, back):
        weight = jnp.where(pick.transpose(2, 0, 1), gate_dup[:, :, None], 0.0)
        weight = weight.reshape(rows, seq_count * slots)
        high = weight.astype(BF16)
        low = (weight - high.astype(F32)).astype(BF16)
        return jnp.dot(high, back, preferred_element_type=F32) + jnp.dot(
            low, back, preferred_element_type=F32
        )

    mixture = combine(picks[0], a_back) + combine(picks[1], b_back)
    left, right = mixture[:, :share], mixture[:, share:]
    theirs = send_core(jnp.where(c == 0, right, left).astype(BF16))
    mine = jnp.where(c == 0, left, right)
    layer_out = (residual.astype(F32) + mine + theirs.astype(F32)).astype(BF16)

    owner_ext = jnp.concatenate([owners, jnp.full((1,), -1, jnp.int32)])
    label_ids = jnp.arange(short_count + 2, dtype=jnp.int32)
    owner_tok = jnp.sum(
        jnp.where(labels[:, None] == label_ids[None, :], owner_ext[None, :], 0), axis=1
    )
    held = (owner_tok == seq_rank).reshape(seq_count, rows)
    held_b = held.astype(BF16)
    inside = jnp.dot(held_b, before.T, preferred_element_type=F32)
    seq_index = jnp.arange(seq_count, dtype=jnp.int32)
    earlier = (seq_index[:, None] > seq_index[None, :]).astype(BF16)
    sizes = jnp.sum(held.astype(F32), axis=1).astype(BF16)
    ahead = jnp.dot(earlier, sizes[:, None], preferred_element_type=F32)
    slot = jnp.where(held, (inside + ahead).astype(jnp.int32), -1).reshape(1, total)
    cache = fill_cache(slot, kv_all)
    return layer_out, cache


def solution(mesh):
    return jax.shard_map(
        local,
        mesh=mesh,
        in_specs=(
            P("seq", None),
            P(),
            P("seq", None),
            P(),
            P(),
            P(None, "tensor"),
            P(None, "tensor"),
            P("tensor", None),
            P(),
            P(),
            P(None, ("seq", "tensor")),
            P(None, ("seq", "tensor")),
            P(("seq", "tensor"), None),
        ),
        out_specs=(P("seq", "tensor"), P("seq", "tensor")),
        check_vma=False,
    )
```

```python
import functools

import jax
import jax.numpy as jnp
from jax import lax
from jax.experimental import pallas as pl
from jax.experimental.pallas import tpu as pltpu
from jax.sharding import PartitionSpec as P


HEADS = 32
KV_HEADS = 8
HEAD_DIM = 128
EXPERTS = 8
EPS = 1e-05
THETA = 1000000.0
FLOOR = -1e30
NZ = 4
MIB = 1024 * 1024
F32 = jnp.float32
BF16 = jnp.bfloat16


VMEM_SPEC = pl.BlockSpec(memory_space=pltpu.VMEM)
ANY_SPEC = pl.BlockSpec(memory_space=pl.ANY)
HBM_SPEC = pl.BlockSpec(memory_space=pltpu.HBM)
SMEM_SPEC = pl.BlockSpec(memory_space=pltpu.SMEM)


def z_perm(step):
    return [(2 * z + c, 2 * ((z + step) % NZ) + c) for z in range(NZ) for c in range(2)]


def core_perm():
    return [(t, t ^ 1) for t in range(2 * NZ)]


def send_z(value, step):
    return lax.ppermute(value, "tensor", z_perm(step))


def send_core(value):
    return lax.ppermute(value, "tensor", core_perm())


def rotate(values, cosine, sine):
    half = values.shape[-1] // 2
    first = values[..., :half]
    second = values[..., half:]
    return jnp.concatenate(
        [first * cosine - second * sine, second * cosine + first * sine], axis=-1
    )


def attention_kernel(ids, first_ref, q_ref, start_ref, kv_ref, w_hbm, mine_ref, sib_ref, w_ref, sem):
    copy = pltpu.make_async_copy(w_hbm, w_ref, sem)
    copy.start()
    rows, dim = start_ref.shape[0], HEAD_DIM
    group = q_ref.shape[0] // rows
    count = kv_ref.shape[0]
    both = 2 * rows
    inner = lax.broadcasted_iota(jnp.int32, (both, count), 0)
    query = first_ref[0] + jnp.where(inner >= rows, inner - rows, inner)
    key = lax.broadcasted_iota(jnp.int32, (both, count), 1)
    start = jnp.concatenate([start_ref[...], start_ref[...]], axis=0)
    mask = (key <= query) & (key >= start)
    scale = HEAD_DIM ** (-0.5)
    heads = []
    for g in range(0, group, 2):
        q = q_ref[g * rows : (g + 2) * rows, :]
        s = lax.dot_general(
            q, kv_ref[:, :dim], (((1,), (1,)), ((), ())), preferred_element_type=F32
        )
        s = jnp.where(mask, s * scale, FLOOR)
        w = jnp.exp(s - jnp.max(s, axis=1, keepdims=True))
        mass = jnp.sum(w, axis=1, keepdims=True)
        acc = jnp.dot(w.astype(BF16), kv_ref[:, dim:], preferred_element_type=F32)
        acc = (acc / mass).astype(BF16)
        heads += [acc[:rows], acc[rows:]]
    attended = jnp.concatenate(heads, axis=1)
    copy.wait()
    share = mine_ref.shape[2]

    def project(at):
        w = w_ref[:, pl.ds(pl.multiple_of(at * share, share), share)]
        return jnp.dot(attended, w, preferred_element_type=F32)

    def body(d, carry):
        sib_ref[d] = project(ids[4 + d]).astype(BF16)
        mine_ref[d] = project(ids[d])
        return carry

    lax.fori_loop(0, NZ, body, 0)


def attend(ids, first, q, start, kv, w_out, share):
    rows = start.shape[0]
    return pl.pallas_call(
        attention_kernel,
        out_shape=(
            jax.ShapeDtypeStruct((NZ, rows, share), F32),
            jax.ShapeDtypeStruct((NZ, rows, share), BF16),
        ),
        in_specs=[SMEM_SPEC, SMEM_SPEC, VMEM_SPEC, VMEM_SPEC, VMEM_SPEC, HBM_SPEC],
        out_specs=(VMEM_SPEC, VMEM_SPEC),
        scratch_shapes=[pltpu.VMEM(w_out.shape, BF16), pltpu.SemaphoreType.DMA],
        compiler_params=pltpu.CompilerParams(vmem_limit_bytes=24 * MIB),
    )(ids, first, q, start, kv, w_out)


def hidden_kernel(count, ids, gain_ref, *refs):
    pieces, refs = refs[:count], refs[count:]
    copies = []
    if len(refs) > 4:
        sources, act_ref, (gate_ref, up_ref, down_ref), (xs_ref, sems) = (
            refs[:6],
            refs[6],
            refs[7:10],
            refs[10:],
        )
        places = [gate_ref.at[0], up_ref.at[0], gate_ref.at[1], up_ref.at[1]]
        places += [down_ref.at[0], down_ref.at[1]]
        copies = [
            pltpu.make_async_copy(source, ref, sems.at[i])
            for i, (source, ref) in enumerate(zip(sources, places, strict=True))
        ]
    else:
        gate_ref, up_ref, act_ref, xs_ref = refs
    for copy in copies[:3]:
        copy.start()
    rows, share = pieces[0].shape
    half = rows // 2
    width = gate_ref.shape[1]
    tile = 32

    for side in range(2):
        chosen = [(pieces[k], 0, k) for k in range(3)] + [(pieces[3 + side], side * half, 3)]

        def norm(i, carry):
            at_row = pl.multiple_of(side * half + i * tile, tile)
            total = jnp.zeros((tile, share), F32)
            for ref, low, _ in chosen:
                v = ref[pl.ds(pl.multiple_of(at_row - low, tile), tile), :].astype(F32)
                total = total + v * v
            mean = jnp.sum(total, axis=1, keepdims=True) * (1.0 / width)
            scale = lax.rsqrt(mean + EPS)
            for ref, low, k in chosen:
                at = ids[k]
                v = ref[pl.ds(pl.multiple_of(at_row - low, tile), tile), :].astype(F32)
                v = v * scale * gain_ref[pl.ds(at, 1), :]
                column = pl.ds(pl.multiple_of(at * share, share), share)
                xs_ref[pl.ds(at_row, tile), column] = v.astype(BF16)
            return carry

        lax.fori_loop(0, half // tile, norm, 0)

    def arrived(i):
        if copies:
            copies[i].wait()
            if i + 3 < len(copies):
                copies[i + 3].start()

    for k in range(2):
        arrived(2 * k)
        gate = jnp.dot(xs_ref[...], gate_ref[k], preferred_element_type=F32)
        arrived(2 * k + 1)
        up = jnp.dot(xs_ref[...], up_ref[k], preferred_element_type=F32)
        act_ref[k] = (gate / (1.0 + jnp.exp(-gate)) * up).astype(BF16)
    for copy in copies[4:]:
        copy.wait()


def down_kernel(ids, act_ref, down_ref, *outs):
    rows, share = outs[0].shape
    half = rows // 2
    for d, places in ((2, (0, 1)), (1, (2, 0)), (3, (1, 2)), (0, (3, 3))):
        column = pl.ds(pl.multiple_of(ids[4 + d] * share, share), share)
        total = jnp.dot(act_ref[0], down_ref[0, :, column], preferred_element_type=F32)
        total = total + jnp.dot(act_ref[1], down_ref[1, :, column], preferred_element_type=F32)
        total = total.astype(BF16)
        for part in range(2):
            at_row = slice(part * half, (part + 1) * half)
            outs[places[part]][at_row, :] = total[at_row, :]


def expert_call(kernel, inputs, weights, outs, scratch):
    spec = VMEM_SPEC
    if weights[0].ndim == 2:
        kinds = (weights[0], weights[1], weights[4])
        outs += tuple(jax.ShapeDtypeStruct((2,) + w.shape, BF16) for w in kinds)
        scratch = scratch + [pltpu.SemaphoreType.DMA((len(weights),))]
        spec = HBM_SPEC
    return pl.pallas_call(
        kernel,
        out_shape=outs,
        in_specs=[SMEM_SPEC] + [VMEM_SPEC] * (len(inputs) - 1) + [spec] * len(weights),
        out_specs=(VMEM_SPEC,) * len(outs),
        scratch_shapes=scratch,
        compiler_params=pltpu.CompilerParams(vmem_limit_bytes=16 * MIB),
    )(*inputs, *weights)


def hidden(ids, gain, weights, pieces):
    rows = pieces[0].shape[0]
    depth, width = weights[0].shape[-2:]
    return expert_call(
        functools.partial(hidden_kernel, len(pieces)),
        (ids, gain, *pieces),
        weights,
        (jax.ShapeDtypeStruct((2, rows, width), BF16),),
        [pltpu.VMEM((rows, depth), BF16)],
    )


def down(ids, active, weights):
    share = weights[0].shape[-1] // NZ
    outs = (jax.ShapeDtypeStruct((active.shape[1], share), BF16),) * 4
    return expert_call(down_kernel, (ids, active), weights, outs, [])


def in_vmem(value):
    return pltpu.with_memory_space_constraint(value, pltpu.VMEM)


def in_hbm(value):
    return pltpu.with_memory_space_constraint(value, pltpu.HBM)


def split_kernel(below_ref, above_ref, low_ref, high_ref):
    half = low_ref.shape[0]
    low_ref[...] = below_ref[:half, :]
    high_ref[...] = above_ref[half:, :]


def gather_ring(own):
    half = own.shape[0] // 2
    below = in_vmem(send_z(own, 1))
    above = in_vmem(send_z(own, -1))
    low, high = local_call(split_kernel, (below, above), (half, half))
    far_a = in_vmem(send_z(low, 1))
    far_b = in_vmem(send_z(high, -1))
    return [own, below, above, far_a, far_b]


def relay_kernel(relay_ref, below_ref, above_ref, low_ref, high_ref):
    half = low_ref.shape[0]
    low = relay_ref[:half, :].astype(F32) + below_ref[:half, :].astype(F32)
    high = relay_ref[half:, :].astype(F32) + above_ref[half:, :].astype(F32)
    low_ref[...] = low.astype(BF16)
    high_ref[...] = high.astype(BF16)


def end_kernel(rest_ref, below_ref, above_ref, low_ref, high_ref, out_ref):
    half = low_ref.shape[0]
    total = rest_ref[...].astype(F32)
    first = total[:half] + above_ref[:half, :].astype(F32) + low_ref[...].astype(F32)
    second = total[half:] + below_ref[half:, :].astype(F32) + high_ref[...].astype(F32)
    out_ref[:half, :] = first.astype(BF16)
    out_ref[half:, :] = second.astype(BF16)


def local_call(kernel, args, heights):
    share = args[0].shape[1]
    return pl.pallas_call(
        kernel,
        out_shape=tuple(jax.ShapeDtypeStruct((height, share), BF16) for height in heights),
        in_specs=[VMEM_SPEC] * len(args),
        out_specs=(VMEM_SPEC,) * len(heights),
        compiler_params=pltpu.CompilerParams(vmem_limit_bytes=16 * MIB),
    )(*args)


def scatter_ring(up, down, relay, rest):
    rows = up.shape[0]
    half = rows // 2
    from_below = in_vmem(send_z(up, 1))
    from_above = in_vmem(send_z(down, -1))
    low, high = local_call(
        relay_kernel, (in_hbm(relay), from_below, from_above), (half, half)
    )
    low = in_hbm(send_z(in_hbm(low), 1))
    high = in_hbm(send_z(in_hbm(high), -1))
    moved = (from_below, from_above, low, high)
    return local_call(end_kernel, (in_hbm(rest), *moved), (rows,))[0]


def cache_kernel(slot_ref, kv_ref, out_ref):
    rows, total = out_ref.shape[0], kv_ref.shape[0]
    place = pl.program_id(0) * rows + lax.broadcasted_iota(jnp.int32, (rows, total), 0)
    take = jnp.where(place == slot_ref[...], 1.0, 0.0).astype(BF16)
    out_ref[...] = jnp.dot(take, kv_ref[...], preferred_element_type=F32).astype(BF16)


def fill_cache(slot, kv):
    total, width = kv.shape
    rows = 256
    return pl.pallas_call(
        cache_kernel,
        grid=(total // rows,),
        out_shape=jax.ShapeDtypeStruct((total, width), BF16),
        in_specs=[
            pl.BlockSpec((1, total), lambda i: (0, 0)),
            pl.BlockSpec((total, width), lambda i: (0, 0)),
        ],
        out_specs=pl.BlockSpec((rows, width), lambda i: (i, 0)),
        compiler_params=pltpu.CompilerParams(vmem_limit_bytes=12 * MIB),
    )(slot, kv)


def local(
    tokens,
    segment_ids,
    routes,
    owners,
    gain_attn,
    w_query,
    w_kv,
    w_out,
    gain_moe,
    w_router,
    w_gate,
    w_up,
    w_down,
):
    seq_count = lax.axis_size("seq")
    ten_count = lax.axis_size("tensor")
    seq_rank = lax.axis_index("seq").astype(jnp.int32)
    ten_rank = lax.axis_index("tensor").astype(jnp.int32)
    rows, width = tokens.shape
    total = segment_ids.shape[0]
    w_out, w_gate, w_up, w_down = (
        pltpu.with_memory_space_constraint(w, pltpu.HBM) for w in (w_out, w_gate, w_up, w_down)
    )
    share = width // ten_count
    group = HEADS // KV_HEADS
    z = ten_rank // 2
    c = ten_rank - z * 2
    first = seq_rank * rows

    short_count = owners.shape[0] - 1
    labels = jnp.where(segment_ids < 0, short_count + 1, segment_ids)
    my_labels = lax.dynamic_slice_in_dim(labels, first, rows)
    seg_start = jnp.sum((labels[None, :] < my_labels[:, None]).astype(jnp.int32), axis=1)
    position = first + jnp.arange(rows, dtype=jnp.int32) - seg_start

    values = tokens.astype(F32)
    scale = lax.rsqrt(jnp.mean(values * values, axis=-1, keepdims=True) + EPS)
    normed = (values * scale * gain_attn).astype(BF16)
    half_dim = HEAD_DIM // 2
    freqs = THETA ** (-(jnp.arange(half_dim, dtype=F32) * 2.0) / HEAD_DIM)
    angles = position.astype(F32)[:, None] * freqs[None, :]
    cosine = jnp.cos(angles)
    sine = jnp.sin(angles)
    pairs = jnp.dot(normed, w_kv, preferred_element_type=F32)
    keys = rotate(pairs[:, :HEAD_DIM], cosine, sine).astype(BF16)
    kv_own = jnp.concatenate([keys, pairs[:, HEAD_DIM:].astype(BF16)], axis=1)
    queries = jnp.dot(normed, w_query, preferred_element_type=F32)
    q = jnp.concatenate(
        [
            rotate(queries[:, g * HEAD_DIM : (g + 1) * HEAD_DIM], cosine, sine).astype(BF16)
            for g in range(group)
        ],
        axis=0,
    )

    kv_all = lax.all_to_all(
        jnp.broadcast_to(kv_own[None], (seq_count,) + kv_own.shape), "seq", 0, 0, tiled=True
    ).reshape(total, kv_own.shape[1])

    g_sib, u_sib, d_sib = (send_core(w) for w in (w_gate, w_up, w_down))
    g_sib, u_sib, d_sib = (
        pltpu.with_memory_space_constraint(w, pltpu.HBM) for w in (g_sib, u_sib, d_sib)
    )
    weights = [w_gate, w_up, g_sib, u_sib, w_down, d_sib]

    ring = lax.rem(z + jnp.arange(NZ, dtype=jnp.int32), NZ) * 2
    other_c = 1 - c
    out_ids = jnp.concatenate([ring + c, ring + other_c])
    out_mine, out_sib = attend(
        out_ids, first.reshape(1), q, seg_start[:, None], kv_all, w_out, share
    )
    out_sib_r = send_core(out_sib)
    sums = [out_mine[d] + out_sib_r[d].astype(F32) for d in range(NZ)]
    attn_sum = sums[0]
    for d in (1, 3, 2):
        attn_sum = attn_sum + send_z(sums[d].astype(BF16), d).astype(F32)
    own_tokens = lax.dynamic_slice_in_dim(tokens, ten_rank * share, share, 1)
    residual = (own_tokens.astype(F32) + attn_sum).astype(BF16)

    sibling = send_core(residual)
    wide = jnp.where(
        c == 0,
        jnp.concatenate([residual, sibling], axis=1),
        jnp.concatenate([sibling, residual], axis=1),
    )

    slots = rows // 8
    holders = seq_count // EXPERTS
    expert_ids = jnp.arange(EXPERTS, dtype=jnp.int32)
    hit = (routes[:, 0:1] == expert_ids[None, :]) | (routes[:, 1:2] == expert_ids[None, :])
    index = jnp.arange(rows, dtype=jnp.int32)
    before = (index[:, None] > index[None, :]).astype(BF16)
    rank = jnp.dot(before, hit.astype(BF16), preferred_element_type=F32).astype(jnp.int32)
    slot_of = jnp.where(hit, rank, -1)
    slot_dup = jnp.repeat(slot_of.T, holders, axis=0)

    def pack(chunk):
        want = (2 * c + chunk) * slots + jnp.arange(slots, dtype=jnp.int32)
        return slot_dup[:, None, :] == want[None, :, None]

    picks = [pack(0), pack(1)]

    def exchange(flat):
        got = lax.all_to_all(
            flat.reshape(seq_count, slots, 2 * share), "seq", 0, 0, tiled=True
        )
        return got.reshape(seq_count * slots, 2 * share)

    def dispatch(pick):
        flat = pick.reshape(seq_count * slots, rows).astype(BF16)
        return exchange(jnp.dot(flat, wide, preferred_element_type=F32).astype(BF16))

    gain_wide = lax.dynamic_slice_in_dim(gain_moe, z * 2 * share, 2 * share)
    router = lax.dynamic_slice_in_dim(w_router, z * 2 * share, 2 * share)
    wide32 = wide.astype(F32)
    part = jnp.dot(
        wide32 * gain_wide, router, preferred_element_type=F32, precision=lax.Precision.HIGHEST
    )
    square = jnp.sum(wide32 * wide32, axis=1, keepdims=True)
    stats = jnp.concatenate([part, square, jnp.zeros((rows, 7), F32)], axis=1)
    stats = stats + lax.ppermute(stats, "tensor", [(t, t ^ 2) for t in range(ten_count)])
    stats = stats + lax.ppermute(stats, "tensor", [(t, t ^ 4) for t in range(ten_count)])
    logits = stats[:, :EXPERTS] * lax.rsqrt(stats[:, EXPERTS : EXPERTS + 1] / width + EPS)
    picked = routes[:, :, None] == expert_ids[None, None, :]
    chosen = jnp.sum(jnp.where(picked, logits[:, None, :], 0.0), axis=2)
    gates = jax.nn.softmax(chosen, axis=1)
    gate_of = jnp.sum(jnp.where(picked, gates[:, :, None], 0.0), axis=1)
    gate_dup = jnp.repeat(gate_of, holders, axis=1)

    gain_rows = gain_moe.reshape(NZ, 2 * share)
    ids = lax.rem(z + jnp.array([0, 3, 1, 2, 0, 1, 2, 3], jnp.int32), NZ)
    a_own = dispatch(picks[0])
    a_pieces = gather_ring(a_own)
    b_own = dispatch(picks[1])
    b_pieces = gather_ring(b_own)
    a_act, *held = hidden(ids, gain_rows, weights, a_pieces)
    held = [in_vmem(w) for w in held]
    a_out = down(ids, a_act, held[2:])
    (b_act,) = hidden(ids, gain_rows, held[:2], b_pieces)
    b_out = down(ids, b_act, held[2:])
    a_final = scatter_ring(*a_out)
    b_final = scatter_ring(*b_out)
    a_back = exchange(a_final)
    b_back = exchange(b_final)

    def combine(pick, back):
        weight = jnp.where(pick.transpose(2, 0, 1), gate_dup[:, :, None], 0.0)
        weight = weight.reshape(rows, seq_count * slots)
        high = weight.astype(BF16)
        low = (weight - high.astype(F32)).astype(BF16)
        return jnp.dot(high, back, preferred_element_type=F32) + jnp.dot(
            low, back, preferred_element_type=F32
        )

    mixture = combine(picks[0], a_back) + combine(picks[1], b_back)
    left, right = mixture[:, :share], mixture[:, share:]
    theirs = send_core(jnp.where(c == 0, right, left).astype(BF16))
    mine = jnp.where(c == 0, left, right)
    layer_out = (residual.astype(F32) + mine + theirs.astype(F32)).astype(BF16)

    owner_ext = jnp.concatenate([owners, jnp.full((1,), -1, jnp.int32)])
    label_ids = jnp.arange(short_count + 2, dtype=jnp.int32)
    owner_tok = jnp.sum(
        jnp.where(labels[:, None] == label_ids[None, :], owner_ext[None, :], 0), axis=1
    )
    held = (owner_tok == seq_rank).reshape(seq_count, rows)
    held_b = held.astype(BF16)
    inside = jnp.dot(held_b, before.T, preferred_element_type=F32)
    seq_index = jnp.arange(seq_count, dtype=jnp.int32)
    earlier = (seq_index[:, None] > seq_index[None, :]).astype(BF16)
    sizes = jnp.sum(held.astype(F32), axis=1).astype(BF16)
    ahead = jnp.dot(earlier, sizes[:, None], preferred_element_type=F32)
    slot = jnp.where(held, (inside + ahead).astype(jnp.int32), -1).reshape(1, total)
    cache = fill_cache(slot, kv_all)
    return layer_out, cache


def solution(mesh):
    return jax.shard_map(
        local,
        mesh=mesh,
        in_specs=(
            P("seq", None),
            P(),
            P("seq", None),
            P(),
            P(),
            P(None, "tensor"),
            P(None, "tensor"),
            P("tensor", None),
            P(),
            P(),
            P(None, ("seq", "tensor")),
            P(None, ("seq", "tensor")),
            P(("seq", "tensor"), None),
        ),
        out_specs=(P("seq", "tensor"), P("seq", "tensor")),
        check_vma=False,
    )
```

```python
import functools

import jax
import jax.numpy as jnp
from jax import lax
from jax.experimental import pallas as pl
from jax.experimental.pallas import tpu as pltpu
from jax.sharding import PartitionSpec as P


HEADS = 32
KV_HEADS = 8
HEAD_DIM = 128
EXPERTS = 8
EPS = 1e-05
THETA = 1000000.0
FLOOR = -1e30
NZ = 4
MIB = 1024 * 1024
F32 = jnp.float32
BF16 = jnp.bfloat16


VMEM_SPEC = pl.BlockSpec(memory_space=pltpu.VMEM)
ANY_SPEC = pl.BlockSpec(memory_space=pl.ANY)
HBM_SPEC = pl.BlockSpec(memory_space=pltpu.HBM)
SMEM_SPEC = pl.BlockSpec(memory_space=pltpu.SMEM)


def z_perm(step):
    return [(2 * z + c, 2 * ((z + step) % NZ) + c) for z in range(NZ) for c in range(2)]


def core_perm():
    return [(t, t ^ 1) for t in range(2 * NZ)]


def send_z(value, step):
    return lax.ppermute(value, "tensor", z_perm(step))


def send_core(value):
    return lax.ppermute(value, "tensor", core_perm())


def rotate(values, cosine, sine):
    half = values.shape[-1] // 2
    first = values[..., :half]
    second = values[..., half:]
    return jnp.concatenate(
        [first * cosine - second * sine, second * cosine + first * sine], axis=-1
    )


def attention_kernel(ids, first_ref, q_ref, start_ref, kv_ref, w_hbm, mine_ref, sib_ref, w_ref, sem):
    copy = pltpu.make_async_copy(w_hbm, w_ref, sem)
    copy.start()
    rows, dim = start_ref.shape[0], HEAD_DIM
    group = q_ref.shape[0] // rows
    count = kv_ref.shape[0]
    both = 2 * rows
    inner = lax.broadcasted_iota(jnp.int32, (both, count), 0)
    query = first_ref[0] + jnp.where(inner >= rows, inner - rows, inner)
    key = lax.broadcasted_iota(jnp.int32, (both, count), 1)
    start = jnp.concatenate([start_ref[...], start_ref[...]], axis=0)
    mask = (key <= query) & (key >= start)
    scale = HEAD_DIM ** (-0.5)
    heads = []
    for g in range(0, group, 2):
        q = q_ref[g * rows : (g + 2) * rows, :]
        s = lax.dot_general(
            q, kv_ref[:, :dim], (((1,), (1,)), ((), ())), preferred_element_type=F32
        )
        s = jnp.where(mask, s * scale, FLOOR)
        w = jnp.exp(s - jnp.max(s, axis=1, keepdims=True))
        mass = jnp.sum(w, axis=1, keepdims=True)
        acc = jnp.dot(w.astype(BF16), kv_ref[:, dim:], preferred_element_type=F32)
        acc = (acc / mass).astype(BF16)
        heads += [acc[:rows], acc[rows:]]
    attended = jnp.concatenate(heads, axis=1)
    copy.wait()
    share = mine_ref.shape[2]

    def project(at):
        w = w_ref[:, pl.ds(pl.multiple_of(at * share, share), share)]
        return jnp.dot(attended, w, preferred_element_type=F32)

    def body(d, carry):
        sib_ref[d] = project(ids[4 + d]).astype(BF16)
        mine_ref[d] = project(ids[d])
        return carry

    lax.fori_loop(0, NZ, body, 0)


def attend(ids, first, q, start, kv, w_out, share):
    rows = start.shape[0]
    return pl.pallas_call(
        attention_kernel,
        out_shape=(
            jax.ShapeDtypeStruct((NZ, rows, share), F32),
            jax.ShapeDtypeStruct((NZ, rows, share), BF16),
        ),
        in_specs=[SMEM_SPEC, SMEM_SPEC, VMEM_SPEC, VMEM_SPEC, VMEM_SPEC, HBM_SPEC],
        out_specs=(VMEM_SPEC, VMEM_SPEC),
        scratch_shapes=[pltpu.VMEM(w_out.shape, BF16), pltpu.SemaphoreType.DMA],
        compiler_params=pltpu.CompilerParams(vmem_limit_bytes=24 * MIB),
    )(ids, first, q, start, kv, w_out)


def hidden_kernel(count, ids, gain_ref, *refs):
    pieces, refs = refs[:count], refs[count:]
    copies = []
    if len(refs) > 4:
        sources, act_ref, (gate_ref, up_ref, down_ref), (xs_ref, sems) = (
            refs[:6],
            refs[6],
            refs[7:10],
            refs[10:],
        )
        places = [gate_ref.at[0], up_ref.at[0], gate_ref.at[1], up_ref.at[1]]
        places += [down_ref.at[0], down_ref.at[1]]
        copies = [
            pltpu.make_async_copy(source, ref, sems.at[i])
            for i, (source, ref) in enumerate(zip(sources, places, strict=True))
        ]
    else:
        gate_ref, up_ref, act_ref, xs_ref = refs
    for copy in copies[:3]:
        copy.start()
    rows, share = pieces[0].shape
    half = rows // 2
    width = gate_ref.shape[1]
    tile = 32

    for side in range(2):
        chosen = [(pieces[k], 0, k) for k in range(3)] + [(pieces[3 + side], side * half, 3)]

        def norm(i, carry):
            at_row = pl.multiple_of(side * half + i * tile, tile)
            total = jnp.zeros((tile, share), F32)
            for ref, low, _ in chosen:
                v = ref[pl.ds(pl.multiple_of(at_row - low, tile), tile), :].astype(F32)
                total = total + v * v
            mean = jnp.sum(total, axis=1, keepdims=True) * (1.0 / width)
            scale = lax.rsqrt(mean + EPS)
            for ref, low, k in chosen:
                at = ids[k]
                v = ref[pl.ds(pl.multiple_of(at_row - low, tile), tile), :].astype(F32)
                v = v * scale * gain_ref[pl.ds(at, 1), :]
                column = pl.ds(pl.multiple_of(at * share, share), share)
                xs_ref[pl.ds(at_row, tile), column] = v.astype(BF16)
            return carry

        lax.fori_loop(0, half // tile, norm, 0)

    def arrived(i):
        if copies:
            copies[i].wait()
            if i + 3 < len(copies):
                copies[i + 3].start()

    for k in range(2):
        arrived(2 * k)
        gate = jnp.dot(xs_ref[...], gate_ref[k], preferred_element_type=F32)
        arrived(2 * k + 1)
        up = jnp.dot(xs_ref[...], up_ref[k], preferred_element_type=F32)
        act_ref[k] = (gate / (1.0 + jnp.exp(-gate)) * up).astype(BF16)
    for copy in copies[4:]:
        copy.wait()


def down_kernel(ids, act_ref, down_ref, *outs):
    rows, share = outs[0].shape
    half = rows // 2
    for d, places in ((2, (0, 1)), (1, (2, 0)), (3, (1, 2)), (0, (3, 3))):
        column = pl.ds(pl.multiple_of(ids[4 + d] * share, share), share)
        total = jnp.dot(act_ref[0], down_ref[0, :, column], preferred_element_type=F32)
        total = total + jnp.dot(act_ref[1], down_ref[1, :, column], preferred_element_type=F32)
        total = total.astype(BF16)
        for part in range(2):
            at_row = slice(part * half, (part + 1) * half)
            outs[places[part]][at_row, :] = total[at_row, :]


def expert_call(kernel, inputs, weights, outs, scratch):
    spec = VMEM_SPEC
    if weights[0].ndim == 2:
        kinds = (weights[0], weights[1], weights[4])
        outs += tuple(jax.ShapeDtypeStruct((2,) + w.shape, BF16) for w in kinds)
        scratch = scratch + [pltpu.SemaphoreType.DMA((len(weights),))]
        spec = HBM_SPEC
    return pl.pallas_call(
        kernel,
        out_shape=outs,
        in_specs=[SMEM_SPEC] + [VMEM_SPEC] * (len(inputs) - 1) + [spec] * len(weights),
        out_specs=(VMEM_SPEC,) * len(outs),
        scratch_shapes=scratch,
        compiler_params=pltpu.CompilerParams(vmem_limit_bytes=16 * MIB),
    )(*inputs, *weights)


def hidden(ids, gain, weights, pieces):
    rows = pieces[0].shape[0]
    depth, width = weights[0].shape[-2:]
    return expert_call(
        functools.partial(hidden_kernel, len(pieces)),
        (ids, gain, *pieces),
        weights,
        (jax.ShapeDtypeStruct((2, rows, width), BF16),),
        [pltpu.VMEM((rows, depth), BF16)],
    )


def down(ids, active, weights):
    share = weights[0].shape[-1] // NZ
    outs = (jax.ShapeDtypeStruct((active.shape[1], share), BF16),) * 4
    return expert_call(down_kernel, (ids, active), weights, outs, [])


def in_vmem(value):
    return pltpu.with_memory_space_constraint(value, pltpu.VMEM)


def in_hbm(value):
    return pltpu.with_memory_space_constraint(value, pltpu.HBM)


def split_kernel(below_ref, above_ref, low_ref, high_ref):
    half = low_ref.shape[0]
    low_ref[...] = below_ref[:half, :]
    high_ref[...] = above_ref[half:, :]


def gather_ring(own, place):
    half = own.shape[0] // 2
    below = send_z(own, 1)
    above = send_z(own, -1)
    low, high = local_call(split_kernel, (below, above), (half, half))
    far_a = in_vmem(send_z(low, 1))
    far_b = in_vmem(send_z(high, -1))
    return [own, place(below), place(above), far_a, far_b]


def relay_kernel(relay_ref, below_ref, above_ref, low_ref, high_ref):
    half = low_ref.shape[0]
    low = relay_ref[:half, :].astype(F32) + below_ref[:half, :].astype(F32)
    high = relay_ref[half:, :].astype(F32) + above_ref[half:, :].astype(F32)
    low_ref[...] = low.astype(BF16)
    high_ref[...] = high.astype(BF16)


def end_kernel(rest_ref, below_ref, above_ref, low_ref, high_ref, out_ref):
    half = low_ref.shape[0]
    total = rest_ref[...].astype(F32)
    first = total[:half] + above_ref[:half, :].astype(F32) + low_ref[...].astype(F32)
    second = total[half:] + below_ref[half:, :].astype(F32) + high_ref[...].astype(F32)
    out_ref[:half, :] = first.astype(BF16)
    out_ref[half:, :] = second.astype(BF16)


def local_call(kernel, args, heights):
    share = args[0].shape[1]
    return pl.pallas_call(
        kernel,
        out_shape=tuple(jax.ShapeDtypeStruct((height, share), BF16) for height in heights),
        in_specs=[VMEM_SPEC] * len(args),
        out_specs=(VMEM_SPEC,) * len(heights),
        compiler_params=pltpu.CompilerParams(vmem_limit_bytes=16 * MIB),
    )(*args)


def scatter_ring(up, down, relay, rest, place):
    rows = up.shape[0]
    half = rows // 2
    from_below = in_vmem(send_z(up, 1))
    from_above = in_vmem(send_z(down, -1))
    low, high = local_call(
        relay_kernel, (place(relay), from_below, from_above), (half, half)
    )
    low = place(send_z(place(low), 1))
    high = place(send_z(place(high), -1))
    moved = (from_below, from_above, low, high)
    return local_call(end_kernel, (place(rest), *moved), (rows,))[0]


def cache_kernel(slot_ref, kv_ref, out_ref):
    rows, total = out_ref.shape[0], kv_ref.shape[0]
    place = pl.program_id(0) * rows + lax.broadcasted_iota(jnp.int32, (rows, total), 0)
    take = jnp.where(place == slot_ref[...], 1.0, 0.0).astype(BF16)
    out_ref[...] = jnp.dot(take, kv_ref[...], preferred_element_type=F32).astype(BF16)


def fill_cache(slot, kv):
    total, width = kv.shape
    rows = 256
    return pl.pallas_call(
        cache_kernel,
        grid=(total // rows,),
        out_shape=jax.ShapeDtypeStruct((total, width), BF16),
        in_specs=[
            pl.BlockSpec((1, total), lambda i: (0, 0)),
            pl.BlockSpec((total, width), lambda i: (0, 0)),
        ],
        out_specs=pl.BlockSpec((rows, width), lambda i: (i, 0)),
        compiler_params=pltpu.CompilerParams(vmem_limit_bytes=12 * MIB),
    )(slot, kv)


def local(
    tokens,
    segment_ids,
    routes,
    owners,
    gain_attn,
    w_query,
    w_kv,
    w_out,
    gain_moe,
    w_router,
    w_gate,
    w_up,
    w_down,
):
    seq_count = lax.axis_size("seq")
    ten_count = lax.axis_size("tensor")
    seq_rank = lax.axis_index("seq").astype(jnp.int32)
    ten_rank = lax.axis_index("tensor").astype(jnp.int32)
    rows, width = tokens.shape
    total = segment_ids.shape[0]
    w_out, w_gate, w_up, w_down = (
        pltpu.with_memory_space_constraint(w, pltpu.HBM) for w in (w_out, w_gate, w_up, w_down)
    )
    share = width // ten_count
    group = HEADS // KV_HEADS
    z = ten_rank // 2
    c = ten_rank - z * 2
    first = seq_rank * rows

    short_count = owners.shape[0] - 1
    labels = jnp.where(segment_ids < 0, short_count + 1, segment_ids)
    my_labels = lax.dynamic_slice_in_dim(labels, first, rows)
    seg_start = jnp.sum((labels[None, :] < my_labels[:, None]).astype(jnp.int32), axis=1)
    position = first + jnp.arange(rows, dtype=jnp.int32) - seg_start

    values = tokens.astype(F32)
    scale = lax.rsqrt(jnp.mean(values * values, axis=-1, keepdims=True) + EPS)
    normed = (values * scale * gain_attn).astype(BF16)
    half_dim = HEAD_DIM // 2
    freqs = THETA ** (-(jnp.arange(half_dim, dtype=F32) * 2.0) / HEAD_DIM)
    angles = position.astype(F32)[:, None] * freqs[None, :]
    cosine = jnp.cos(angles)
    sine = jnp.sin(angles)
    pairs = jnp.dot(normed, w_kv, preferred_element_type=F32)
    keys = rotate(pairs[:, :HEAD_DIM], cosine, sine).astype(BF16)
    kv_own = jnp.concatenate([keys, pairs[:, HEAD_DIM:].astype(BF16)], axis=1)
    queries = jnp.dot(normed, w_query, preferred_element_type=F32)
    q = jnp.concatenate(
        [
            rotate(queries[:, g * HEAD_DIM : (g + 1) * HEAD_DIM], cosine, sine).astype(BF16)
            for g in range(group)
        ],
        axis=0,
    )

    kv_all = lax.all_to_all(
        jnp.broadcast_to(kv_own[None], (seq_count,) + kv_own.shape), "seq", 0, 0, tiled=True
    ).reshape(total, kv_own.shape[1])

    g_sib, u_sib, d_sib = (send_core(w) for w in (w_gate, w_up, w_down))
    g_sib, u_sib, d_sib = (
        pltpu.with_memory_space_constraint(w, pltpu.HBM) for w in (g_sib, u_sib, d_sib)
    )
    weights = [w_gate, w_up, g_sib, u_sib, w_down, d_sib]

    ring = lax.rem(z + jnp.arange(NZ, dtype=jnp.int32), NZ) * 2
    other_c = 1 - c
    out_ids = jnp.concatenate([ring + c, ring + other_c])
    out_mine, out_sib = attend(
        out_ids, first.reshape(1), q, seg_start[:, None], kv_all, w_out, share
    )
    out_sib_r = send_core(out_sib)
    sums = [out_mine[d] + out_sib_r[d].astype(F32) for d in range(NZ)]
    attn_sum = sums[0]
    for d in (1, 3, 2):
        attn_sum = attn_sum + send_z(sums[d].astype(BF16), d).astype(F32)
    own_tokens = lax.dynamic_slice_in_dim(tokens, ten_rank * share, share, 1)
    residual = (own_tokens.astype(F32) + attn_sum).astype(BF16)

    sibling = send_core(residual)
    wide = jnp.where(
        c == 0,
        jnp.concatenate([residual, sibling], axis=1),
        jnp.concatenate([sibling, residual], axis=1),
    )

    slots = rows // 8
    holders = seq_count // EXPERTS
    expert_ids = jnp.arange(EXPERTS, dtype=jnp.int32)
    hit = (routes[:, 0:1] == expert_ids[None, :]) | (routes[:, 1:2] == expert_ids[None, :])
    index = jnp.arange(rows, dtype=jnp.int32)
    before = (index[:, None] > index[None, :]).astype(BF16)
    rank = jnp.dot(before, hit.astype(BF16), preferred_element_type=F32).astype(jnp.int32)
    slot_of = jnp.where(hit, rank, -1)
    slot_dup = jnp.repeat(slot_of.T, holders, axis=0)

    def pack(chunk):
        want = (2 * c + chunk) * slots + jnp.arange(slots, dtype=jnp.int32)
        return slot_dup[:, None, :] == want[None, :, None]

    picks = [pack(0), pack(1)]

    def exchange(flat):
        got = lax.all_to_all(
            flat.reshape(seq_count, slots, 2 * share), "seq", 0, 0, tiled=True
        )
        return got.reshape(seq_count * slots, 2 * share)

    def dispatch(pick):
        flat = pick.reshape(seq_count * slots, rows).astype(BF16)
        return exchange(jnp.dot(flat, wide, preferred_element_type=F32).astype(BF16))

    gain_wide = lax.dynamic_slice_in_dim(gain_moe, z * 2 * share, 2 * share)
    router = lax.dynamic_slice_in_dim(w_router, z * 2 * share, 2 * share)
    wide32 = wide.astype(F32)
    part = jnp.dot(
        wide32 * gain_wide, router, preferred_element_type=F32, precision=lax.Precision.HIGHEST
    )
    square = jnp.sum(wide32 * wide32, axis=1, keepdims=True)
    stats = jnp.concatenate([part, square, jnp.zeros((rows, 7), F32)], axis=1)
    stats = stats + lax.ppermute(stats, "tensor", [(t, t ^ 2) for t in range(ten_count)])
    stats = stats + lax.ppermute(stats, "tensor", [(t, t ^ 4) for t in range(ten_count)])
    logits = stats[:, :EXPERTS] * lax.rsqrt(stats[:, EXPERTS : EXPERTS + 1] / width + EPS)
    picked = routes[:, :, None] == expert_ids[None, None, :]
    chosen = jnp.sum(jnp.where(picked, logits[:, None, :], 0.0), axis=2)
    gates = jax.nn.softmax(chosen, axis=1)
    gate_of = jnp.sum(jnp.where(picked, gates[:, :, None], 0.0), axis=1)
    gate_dup = jnp.repeat(gate_of, holders, axis=1)

    gain_rows = gain_moe.reshape(NZ, 2 * share)
    ids = lax.rem(z + jnp.array([0, 3, 1, 2, 0, 1, 2, 3], jnp.int32), NZ)
    a_own = dispatch(picks[0])
    a_pieces = gather_ring(a_own, in_hbm)
    b_own = dispatch(picks[1])
    b_pieces = gather_ring(b_own, in_vmem)
    a_act, *held = hidden(ids, gain_rows, weights, a_pieces)
    held = [in_vmem(w) for w in held]
    a_out = down(ids, a_act, held[2:])
    (b_act,) = hidden(ids, gain_rows, held[:2], b_pieces)
    b_out = down(ids, b_act, held[2:])
    a_final = scatter_ring(*a_out, in_vmem)
    b_final = scatter_ring(*b_out, in_hbm)
    a_back = exchange(a_final)
    b_back = exchange(b_final)

    def combine(pick, back):
        weight = jnp.where(pick.transpose(2, 0, 1), gate_dup[:, :, None], 0.0)
        weight = weight.reshape(rows, seq_count * slots)
        high = weight.astype(BF16)
        low = (weight - high.astype(F32)).astype(BF16)
        return jnp.dot(high, back, preferred_element_type=F32) + jnp.dot(
            low, back, preferred_element_type=F32
        )

    mixture = lax.optimization_barrier(combine(picks[0], a_back)) + combine(picks[1], b_back)
    left, right = mixture[:, :share], mixture[:, share:]
    theirs = send_core(jnp.where(c == 0, right, left).astype(BF16))
    mine = jnp.where(c == 0, left, right)
    layer_out = (residual.astype(F32) + mine + theirs.astype(F32)).astype(BF16)

    owner_ext = jnp.concatenate([owners, jnp.full((1,), -1, jnp.int32)])
    label_ids = jnp.arange(short_count + 2, dtype=jnp.int32)
    owner_tok = jnp.sum(
        jnp.where(labels[:, None] == label_ids[None, :], owner_ext[None, :], 0), axis=1
    )
    held = (owner_tok == seq_rank).reshape(seq_count, rows)
    held_b = held.astype(BF16)
    inside = jnp.dot(held_b, before.T, preferred_element_type=F32)
    seq_index = jnp.arange(seq_count, dtype=jnp.int32)
    earlier = (seq_index[:, None] > seq_index[None, :]).astype(BF16)
    sizes = jnp.sum(held.astype(F32), axis=1).astype(BF16)
    ahead = jnp.dot(earlier, sizes[:, None], preferred_element_type=F32)
    slot = jnp.where(held, (inside + ahead).astype(jnp.int32), -1).reshape(1, total)
    cache = fill_cache(slot, kv_all)
    return layer_out, cache


def solution(mesh):
    return jax.shard_map(
        local,
        mesh=mesh,
        in_specs=(
            P("seq", None),
            P(),
            P("seq", None),
            P(),
            P(),
            P(None, "tensor"),
            P(None, "tensor"),
            P("tensor", None),
            P(),
            P(),
            P(None, ("seq", "tensor")),
            P(None, ("seq", "tensor")),
            P(("seq", "tensor"), None),
        ),
        out_specs=(P("seq", "tensor"), P("seq", "tensor")),
        check_vma=False,
    )
```
